32 devices in a mesh: depth: 8 (over y, x, core), tile: 4 (over z).
Axes of the slice: x: 2, y: 2, z: 4, core: 2. Of those that a mesh axis runs over, the one named last changes fastest.
Arguments:
- fronts: float32 [8, 4, 8, 2, 128, 128], P('depth', 'tile'), may hold values from -6 to 6
- probe_wave: float32 [2, 128, 128], replicated, may hold values from -6 to 6
- object_slices: bfloat16 [16, 2, 1536, 384], P('depth', None, 'tile')
- patch_list: int32 [11, 4, 3, 8], P(None, 'tile'), may hold values from 0 to 256, as said below
- counts: int32 [11, 4], P(None, 'tile'), may hold values from 1 to 8, as said below
Outputs:
- exit_waves: float32 [8, 4, 8, 2, 128, 128], P('depth', 'tile')
The draws below stay inside these ranges and needn't reach their ends.
Inputs may be any that keep to these rules, and one draw needn't show every extreme that they name: `patch_list`: rows and columns of corners run from 0 to 256, and that end is reached. Among the live probes of one batch of one owner no tile is named more than 2 times; a batch of 8 probes names every tile exactly 2 times. `counts`: some batch of some owner holds 8 probes.
All inputs are finite; a program needn't handle non-finite values.
Results may differ from the reference program's by a relative error of at most 0.0003.
Values may be sent and summed in bfloat16 or wider, within the bound.
No kernel may reach another device: no remote copies, remote signals or barrier semaphores. Data moves between devices by JAX's collectives and lax.ppermute only.
A program may use at most 64 MiB of HBM per device.

```python
import math
import jax
import jax.numpy as jnp
from jax import lax

W = 128
TSIDE = 384
SLOTS = 8
STEPS = 4
SLICES = 16
BATCHES = 11
REGION = 1536
N_DEPTH = 8
N_TILE = 4


def draw_object_slices(key, part):
    shape = (SLICES, REGION, TSIDE)
    first_key = jax.random.fold_in(key, 31)
    second_key = jax.random.fold_in(key, 32)
    amplitude = jax.random.uniform(first_key, shape, jnp.float32, 0.8, 1.0)
    phase = jax.random.uniform(second_key, shape, jnp.float32, -math.pi, math.pi)
    return jnp.stack([amplitude * jnp.cos(phase), amplitude * jnp.sin(phase)], axis=1).astype(jnp.bfloat16)


def draw_counts(key, part):
    upper = max(2, 2 * SLOTS // 3)
    base = jax.random.randint(jax.random.fold_in(key, 11), (BATCHES * N_TILE,), 1, upper + 1, dtype=jnp.int32)
    location = jax.random.randint(jax.random.fold_in(key, 12), (), 0, BATCHES * N_TILE, dtype=jnp.int32)
    base = base.at[location].set(SLOTS)
    return base.reshape(BATCHES, N_TILE)


def draw_patch_list(key, part):
    pair = SLOTS // N_TILE
    keys = jax.random.split(jax.random.fold_in(key, 21), BATCHES * N_TILE)
    orders = jax.vmap(lambda one: jax.random.permutation(one, SLOTS))(keys).astype(jnp.int32)
    tile_ids = (orders // pair).reshape(BATCHES, N_TILE, SLOTS)
    row_start = jax.random.randint(jax.random.fold_in(key, 22), (BATCHES * N_TILE * SLOTS,), 0, TSIDE - W + 1, dtype=jnp.int32)
    location = jax.random.randint(jax.random.fold_in(key, 23), (), 0, BATCHES * N_TILE * SLOTS, dtype=jnp.int32)
    row_start = row_start.at[location].set(TSIDE - W).reshape(BATCHES, N_TILE, SLOTS)
    column_start = jax.random.randint(jax.random.fold_in(key, 24), (BATCHES, N_TILE, SLOTS), 0, TSIDE - W + 1, dtype=jnp.int32)
    return jnp.stack([tile_ids, row_start, column_start], axis=2)


def level_of(rng, extent, cuts, low, largest):
    def one(position, parts):
        draws = jax.random.uniform(jax.random.fold_in(jax.random.fold_in(rng, 6), position), (parts,), jnp.float32, low / len(cuts), largest / len(cuts))
        return jnp.repeat(jnp.exp(draws), extent[position] // parts).reshape((-1,) + (1,) * (len(extent) - position - 1))

    factor_of = one(*cuts[0])
    for cut in cuts[1:]:
        factor_of = factor_of * one(*cut)
    return factor_of


def noise(stream_key, extent, scale, limit, cuts=(), held_as=jnp.bfloat16):
    drawn = jax.random.normal(stream_key, extent, jnp.float32) * scale
    if len(cuts) > 0:
        drawn = level_of(stream_key, extent, cuts, -0.22, 0.18) * drawn
    return jnp.clip(drawn, min=-limit, max=limit).astype(held_as)


def setup_inputs(seed: int = 0) -> dict:
    splits = jax.random.split(jax.random.key(seed), 6)
    fronts = noise(splits[0], (N_DEPTH, N_TILE, SLOTS, 2, W, W), 1.0, 6.0, ((0, 8), (1, 4)), jnp.float32)
    probe_wave = noise(splits[1], (2, W, W), 1.0, 6.0, (), jnp.float32)
    object_slices = draw_object_slices(jax.random.fold_in(splits[5], 71), 0)
    patch_list = draw_patch_list(jax.random.fold_in(splits[5], 71), 0)
    counts = draw_counts(jax.random.fold_in(splits[5], 71), 0)
    return {"fronts": fronts, "probe_wave": probe_wave, "object_slices": object_slices, "patch_list": patch_list, "counts": counts}


fresnel_rate = 0.3


def dft_tables(width, inverse):
    index = jnp.arange(width, dtype=jnp.int32)
    angle = (2.0 * math.pi / width) * ((index[:, None] * index[None, :]) % width).astype(jnp.float32)
    cosine = jnp.cos(angle)
    sine = jnp.sin(angle)
    if inverse:
        cosine = cosine / width
        imagine = sine / width
    else:
        imagine = -sine
    return (cosine, cosine + imagine, imagine - cosine)


def plane_dot(plane, table):
    shape = plane.shape
    flat = plane.reshape(-1, shape[-1])
    return jnp.dot(flat, table, precision=lax.Precision.HIGHEST, preferred_element_type=jnp.float32).reshape(shape)


def right_multiply(real_part, imag_part, tables):
    cosine, summed, differ = tables
    first = plane_dot(real_part + imag_part, cosine)
    second = plane_dot(real_part, differ)
    third = plane_dot(imag_part, summed)
    return first - third, first + second


def transform(real_part, imag_part, tables):
    real_part, imag_part = right_multiply(real_part, imag_part, tables)
    return right_multiply(jnp.swapaxes(real_part, -1, -2), jnp.swapaxes(imag_part, -1, -2), tables)


def fresnel(width):
    index = jnp.arange(width, dtype=jnp.int32)
    freq = jnp.where(index < width // 2, index, index - width).astype(jnp.float32)
    phase = (-2.0 * math.pi * fresnel_rate / width) * (freq[:, None] ** 2 + freq[None, :] ** 2)
    return jnp.cos(phase), jnp.sin(phase)


def slab_pass(wavefield, patches):
    width = wavefield.shape[-1]
    forward = dft_tables(width, False)
    backward = dft_tables(width, True)
    kernel_cos, kernel_sin = fresnel(width)
    real_part = wavefield[:, 0]
    imag_part = wavefield[:, 1]
    for layer in range(2):
        trans_real = patches[:, layer, 0].astype(jnp.float32)
        trans_imag = patches[:, layer, 1].astype(jnp.float32)
        real_part, imag_part = real_part * trans_real - imag_part * trans_imag, real_part * trans_imag + imag_part * trans_real
        spec_real, spec_imag = transform(real_part, imag_part, forward)
        spec_real, spec_imag = spec_real * kernel_cos - spec_imag * kernel_sin, spec_real * kernel_sin + spec_imag * kernel_cos
        real_part, imag_part = transform(spec_real, spec_imag, backward)
    return jnp.stack([real_part, imag_part], axis=1)


def reference(fronts, probe_wave, object_slices, patch_list, counts):
    slot_index = jnp.arange(SLOTS, dtype=jnp.int32)

    def one_slab(depth_index):
        batch = (N_DEPTH + STEPS - 2 - depth_index).astype(jnp.int32)
        listing = lax.dynamic_index_in_dim(patch_list, batch, 0, keepdims=False)
        count_row = lax.dynamic_index_in_dim(counts, batch, 0, keepdims=False)
        live = (slot_index[None, :] < count_row[:, None]).astype(jnp.float32)
        source = jnp.maximum(depth_index - STEPS + 1, 0).astype(jnp.int32)
        held = lax.dynamic_index_in_dim(fronts, source, 0, keepdims=False)
        start = jnp.where(depth_index >= STEPS - 1, held, probe_wave[None, None]) * live[:, :, None, None, None]
        wavefield = start.reshape(N_TILE * SLOTS, 2, W, W)
        row_start = (listing[:, 0] * TSIDE + listing[:, 1]).reshape(-1).astype(jnp.int32)
        column_start = listing[:, 2].reshape(-1).astype(jnp.int32)
        for section in range(STEPS):
            slab = depth_index - STEPS + 1 + section
            layers = lax.dynamic_slice_in_dim(object_slices, (2 * jnp.maximum(slab, 0)).astype(jnp.int32), 2, 0)

            def cut_patch(row_value, column_value):
                zero = jnp.zeros((), jnp.int32)
                return lax.dynamic_slice(layers, (zero, zero, row_value, column_value), (2, 2, W, W))

            patches = jax.vmap(cut_patch)(row_start, column_start)
            moved = slab_pass(wavefield, patches)
            wavefield = jnp.where(slab >= 0, moved, wavefield)
        return wavefield.reshape(N_TILE, SLOTS, 2, W, W)

    return lax.map(one_slab, jnp.arange(N_DEPTH, dtype=jnp.int32))
```

```python
import functools
import math

import jax
import jax.numpy as jnp
import ml_dtypes
import numpy as np
from jax import lax
from jax.experimental import pallas as pl
from jax.experimental.pallas import tpu as pltpu
from jax.sharding import PartitionSpec as P

STEPS = 4
FRESNEL_RATE = 0.3
EXTRA = 16
GROUP = 4

ANY = pl.BlockSpec(memory_space=pl.ANY)
VMEM = pl.BlockSpec(memory_space=pltpu.VMEM)
SMEM = pl.BlockSpec(memory_space=pltpu.SMEM)


def halves(table):
    high = table.astype(ml_dtypes.bfloat16)
    low = (table - high.astype(np.float64)).astype(ml_dtypes.bfloat16)
    return high, low


@functools.lru_cache(None)
def propagators(width):
    index = np.arange(width)
    angle = 2.0 * np.pi * ((index[:, None] * index[None, :]) % width) / width
    freq = np.where(index < width // 2, index, index - width).astype(np.float64)
    factor = np.exp(-2j * np.pi * FRESNEL_RATE / width * freq**2)
    step = (np.exp(1j * angle) / width) @ (factor[:, None] * np.exp(-1j * angle))
    right = np.block([[step.real, step.imag], [-step.imag, step.real]])
    right_high, right_low = halves(right)
    left_high, left_low = halves(right.T)
    right3 = np.concatenate([right_high, right_high, right_low], axis=0)
    left3 = np.concatenate([left_high, left_high, left_low], axis=1)
    return right3, left3


def split(value):
    high = value.astype(jnp.bfloat16)
    low = (value - high.astype(jnp.float32)).astype(jnp.bfloat16)
    return high, low


def encode(real, imag, store):
    width = real.shape[0]
    codes = []
    for plane, value in enumerate((real, imag)):
        top = jnp.maximum(jnp.max(jnp.abs(value), axis=0, keepdims=True), 2.0**-100)
        code = jnp.ceil((jnp.log(top * (1.0 / 32766.0)) * (256.0 / math.log(2.0))))
        store(plane * width, jnp.round(value * jnp.exp2(code * (-1.0 / 256.0))).astype(jnp.int32).astype(jnp.int16))
        codes.append(jnp.broadcast_to(code, (EXTRA // 2, code.shape[1])))
    store(2 * width, jnp.concatenate(codes, axis=0).astype(jnp.int32).astype(jnp.int16))


def decode(load, width):
    scales = jnp.exp2(load(2 * width, EXTRA).astype(jnp.int32).astype(jnp.float32) * (1.0 / 256.0))
    real = load(0, width).astype(jnp.int32).astype(jnp.float32) * scales[0:1]
    imag = load(width, width).astype(jnp.int32).astype(jnp.float32) * scales[EXTRA // 2 : EXTRA // 2 + 1]
    return real, imag


def nth_of_tile(tile_of, count, slots, tile, nth):
    found = jnp.int32(-1)
    seen = jnp.int32(0)
    for p in range(slots):
        hit = (tile_of(p) == tile) & (p < count)
        found = jnp.where(hit & (seen == nth), p, found)
        seen = seen + hit.astype(jnp.int32)
    return found


def pack_kernel(tiles, pair, meta_ref, fronts_ref, *out_refs):
    slots, _, width, _ = fronts_ref.shape
    own = lax.axis_index("tile")
    batch = lax.axis_size("depth") - 1 - lax.axis_index("depth")
    count = meta_ref[batch, 3 * slots]
    for k in range(tiles):
        tile = lax.rem(own + k, tiles)
        for i in range(pair):
            p = nth_of_tile(lambda p: meta_ref[batch, p], count, slots, tile, i)

            @pl.when(p >= 0)
            def _():
                def store(row, block):
                    out_refs[k][i, row : row + block.shape[0], :] = block

                encode(fronts_ref[p, 0], fronts_ref[p, 1], store)


def unpack_kernel(tiles, pair, meta_ref, *refs):
    in_refs, out_ref = refs[:tiles], refs[tiles]
    slots, _, width, _ = out_ref.shape
    own = lax.axis_index("tile")
    batch = lax.axis_size("depth") + STEPS - 2 - lax.axis_index("depth")
    count = meta_ref[batch, 3 * slots]
    for p in range(slots):

        @pl.when(p >= count)
        def _():
            out_ref[p] = jnp.zeros(out_ref.shape[1:], jnp.float32)

    for k in range(tiles):
        tile = lax.rem(own + k, tiles)
        for i in range(pair):
            p = nth_of_tile(lambda p: meta_ref[batch, p], count, slots, tile, i)

            @pl.when(p >= 0)
            def _():
                real, imag = decode(lambda row, size: in_refs[k][i, row : row + size, :], width)
                out_ref[p, 0] = real
                out_ref[p, 1] = imag


def cut(tile_ref, which, plane, row, block, shift, width):
    turn = lax.rem(width - shift, width)
    left = pltpu.roll(tile_ref[which, plane, block, pl.ds(row, width), :], turn, 1)
    right = pltpu.roll(tile_ref[which, plane, block + 1, pl.ds(row, width), :], turn, 1)
    lane = lax.broadcasted_iota(jnp.int32, (width, width), 1)
    return jnp.where(lane < width - shift, left, right)


def layer_pass(width, tile_ref, which, places, x_refs, wave_ref, y_refs, right_ref, left_ref):
    for w in range(GROUP):
        row, block, shift = places[w]
        trans_real = cut(tile_ref, which, 0, row, block, shift, width)
        trans_imag = cut(tile_ref, which, 1, row, block, shift, width)
        rows = slice(w * width, (w + 1) * width)
        real, imag = wave_ref[rows, :width], wave_ref[rows, width:]
        for plane, value in enumerate((real * trans_real - imag * trans_imag, real * trans_imag + imag * trans_real)):
            high, low = split(value)
            x_refs[rows, plane * width : (plane + 1) * width] = high
            x_refs[rows, (2 + plane) * width : (3 + plane) * width] = low
            x_refs[rows, (4 + plane) * width : (5 + plane) * width] = high
    for w in range(GROUP):
        rows = slice(w * width, (w + 1) * width)
        spread = jnp.dot(x_refs[rows, :], right_ref[...], preferred_element_type=jnp.float32)
        high, low = split(spread)
        side = slice((w % 2) * width, (w % 2 + 1) * width)
        for plane in range(2):
            lanes = slice(plane * width, (plane + 1) * width)
            y_refs[w // 2, plane * width : (plane + 1) * width, side] = high[:, lanes]
            y_refs[w // 2, (2 + plane) * width : (3 + plane) * width, side] = low[:, lanes]
            y_refs[w // 2, (4 + plane) * width : (5 + plane) * width, side] = high[:, lanes]
    for g in range(GROUP // 2):
        out = jnp.dot(left_ref[...], y_refs[g], preferred_element_type=jnp.float32)
        for w in range(2):
            rows = slice((2 * g + w) * width, (2 * g + w + 1) * width)
            side = slice(w * width, (w + 1) * width)
            wave_ref[rows, :width] = out[:width, side]
            wave_ref[rows, width:] = out[width:, side]


def stage_kernel(stage, tiles, pair, *refs):
    names = 4 + (tiles if stage == 0 else 2)
    metas = refs[:tiles]
    own_ref, near_ref, far_ref, right_ref, left_ref = refs[tiles : tiles + 5]
    rest = refs[tiles + 5 :]
    if stage == 0:
        in_refs, rest = rest[:tiles], rest[tiles:]
        probe_ref, move_ref, keep_ref = rest[:3]
        rest = rest[3:]
    else:
        arrived_ref, keep_ref, probe_ref = rest[:3]
        out_refs = rest[3 : 3 + tiles]
        rest = rest[3 + tiles :]
    bf_ref, tile_ref, waves_ref, wave_ref, x_ref, y_ref, row_ref, column_ref, slot_ref, sems = rest
    slots = metas[0].shape[1] // 4
    width = probe_ref.shape[-1]
    depth = lax.axis_index("depth")
    depths = lax.axis_size("depth")
    own = lax.axis_index("tile")
    odd = lax.rem(depth, 2) == 1
    if stage == 0:
        batch = jnp.where(odd, depths + 1 - depth, depths - 1 - depth)
        exists = jnp.where(odd, depth < depths - 1, depth + STEPS - 1 < depths)
        first_on = jnp.logical_or(jnp.logical_not(odd), depth > 1)
        from_probe = odd & (depth == 1)
    else:
        batch = jnp.where(odd & (depth == depths - 1), depths + 2, depths + 1 - depth)
        exists = jnp.bool_(True)
        first_on = depth < depths - 1
        from_probe = jnp.logical_or(depth == 0, depth == depths - 1)

    @pl.when(exists)
    def _():
        def fetch(source, slot):
            return pltpu.make_async_copy(source, bf_ref.at[slot], sems.at[slot])

        if stage == 0:

            @pl.when(odd)
            def _():
                fetch(far_ref, 0).start()

            @pl.when(jnp.logical_not(odd))
            def _():
                fetch(own_ref, 0).start()

            fetch(near_ref, 1).start()
        else:
            fetch(own_ref, 0).start()

            @pl.when(odd)
            def _():
                fetch(far_ref, 1).start()

            @pl.when(jnp.logical_not(odd))
            def _():
                fetch(near_ref, 1).start()

        if stage == 0:
            bring = [
                pltpu.make_async_copy(in_refs[k], waves_ref.at[pl.ds(k * pair, pair)], sems.at[2 + k])
                for k in range(tiles)
            ]
        else:
            bring = [pltpu.make_async_copy(arrived_ref, waves_ref, sems.at[2])]
        for copy in bring:
            copy.start()
        total = jnp.int32(0)
        for j in range(tiles * pair):
            slot_ref[j] = 0
            row_ref[j] = 0
            column_ref[j] = 0
        for k in range(tiles):
            count = metas[k][batch, 3 * slots]
            seen = jnp.int32(0)
            for p in range(slots):
                hit = ((metas[k][batch, p] == own) & (p < count)).astype(jnp.int32)

                @pl.when(hit == 1)
                def _():
                    slot_ref[total] = k * pair + seen
                    row_ref[total] = metas[k][batch, slots + p]
                    column_ref[total] = metas[k][batch, 2 * slots + p]

                total = total + hit
                seen = seen + hit
        for slot in range(2):
            fetch(own_ref, slot).wait()
        for copy in bring:
            copy.wait()
        planes = [(s, l, q) for s in range(2) for l in range(2) for q in range(2)]
        for s, l, q in planes:
            for b in range(tile_ref.shape[2]):
                tile_ref[2 * s + l, q, b] = bf_ref[s, l, q, :, b * width : (b + 1) * width].astype(jnp.float32)

        def group(g, carry):
            places = []
            for w in range(GROUP):
                j = g * GROUP + w
                column = column_ref[j]
                block = jnp.minimum(column // width, bf_ref.shape[-1] // width - 2)
                places.append((row_ref[j], block, column - block * width))
                rows = slice(w * width, (w + 1) * width)
                slot = slot_ref[j]

                def load_coded():
                    real, imag = decode(lambda row, size: waves_ref[slot, row : row + size, :], width)
                    wave_ref[rows, :width] = real
                    wave_ref[rows, width:] = imag

                def load_probe():
                    wave_ref[rows, :width] = probe_ref[0]
                    wave_ref[rows, width:] = probe_ref[1]

                pl.when(from_probe)(load_probe)
                if stage == 0:
                    pl.when(jnp.logical_not(from_probe))(load_coded)
                else:
                    def load_kept():
                        wave_ref[rows, :width] = keep_ref[slot, 0]
                        wave_ref[rows, width:] = keep_ref[slot, 1]

                    pl.when(jnp.logical_not(from_probe) & odd)(load_kept)
                    pl.when(jnp.logical_not(from_probe) & jnp.logical_not(odd))(load_coded)

            def one_layer(which, carry):
                layer_pass(width, tile_ref, which, places, x_ref, wave_ref, y_ref, right_ref, left_ref)
                return carry

            lax.fori_loop(jnp.where(first_on, 0, 2), 4, one_layer, 0)
            for w in range(GROUP):
                j = g * GROUP + w

                @pl.when(j < total)
                def _():
                    slot = slot_ref[j]
                    rows = slice(w * width, (w + 1) * width)
                    real, imag = wave_ref[rows, :width], wave_ref[rows, width:]
                    if stage == 0:

                        @pl.when(odd)
                        def _():
                            keep_ref[slot, 0] = real
                            keep_ref[slot, 1] = imag

                        @pl.when(jnp.logical_not(odd))
                        def _():
                            def store(row, block):
                                move_ref[slot, row : row + block.shape[0], :] = block

                            encode(real, imag, store)
                    else:

                        def store(row, block):
                            waves_ref[slot, row : row + block.shape[0], :] = block

                        encode(real, imag, store)

            return carry

        lax.fori_loop(0, (total + GROUP - 1) // GROUP, group, 0)
        if stage == 1:
            for k in range(tiles):
                out_refs[k][...] = waves_ref[k * pair : (k + 1) * pair]


def per_device(fronts, probe_wave, object_slices, patch_list, counts):
    depths = lax.axis_size("depth")
    tiles = lax.axis_size("tile")
    slots = fronts.shape[2]
    width = fronts.shape[-1]
    side = object_slices.shape[-1]
    pair = slots // tiles
    right3, left3 = (jnp.asarray(table) for table in propagators(width))
    both = ("depth", "tile")

    def flat(depth, tile):
        return (depth % depths) * tiles + tile % tiles

    meta = jnp.concatenate(
        [patch_list[:, 0].reshape(patch_list.shape[0], -1), jnp.broadcast_to(counts, (counts.shape[0], slots))], axis=1
    )
    metas = [meta] + [lax.ppermute(meta, "tile", [(t, (t + k) % tiles) for t in range(tiles)]) for k in range(1, tiles)]
    near = lax.ppermute(object_slices, "depth", [(d, d ^ 1) for d in range(depths)])
    below = lax.ppermute(object_slices, "depth", [(d, d + 2) for d in range(1, depths - 2, 2)])
    above = lax.ppermute(object_slices, "depth", [((d + 1) % depths, d) for d in range(1, depths, 2)])
    coded = jax.ShapeDtypeStruct((pair, 2 * width + EXTRA, width), jnp.int16)
    all_coded = jax.ShapeDtypeStruct((tiles * pair, 2 * width + EXTRA, width), jnp.int16)
    packed = pl.pallas_call(
        functools.partial(pack_kernel, tiles, pair),
        out_shape=[coded] * tiles,
        in_specs=[SMEM, VMEM],
        out_specs=[VMEM] * tiles,
        name="pack",
    )(meta, fronts[0, 0])
    brought = []
    for k in range(tiles):
        pairs = []
        for t in range(tiles):
            pairs += [(flat(d, t), flat(d, t + k)) for d in range(0, depths - STEPS + 1, 2)]
            pairs += [(flat(d, t), flat(d + 2, t + k)) for d in range(1, depths - STEPS, 2)]
        brought.append(lax.ppermute(packed[k], both, pairs))
    slab = object_slices.shape

    def scratch():
        return [
            pltpu.VMEM((2,) + slab, jnp.bfloat16),
            pltpu.VMEM((4, 2, side // width, side, width), jnp.float32),
            pltpu.VMEM(all_coded.shape, jnp.int16),
            pltpu.VMEM((GROUP * width, 2 * width), jnp.float32),
            pltpu.VMEM((GROUP * width, 6 * width), jnp.bfloat16),
            pltpu.VMEM((GROUP // 2, 6 * width, 2 * width), jnp.bfloat16),
            pltpu.SMEM((tiles * pair,), jnp.int32),
            pltpu.SMEM((tiles * pair,), jnp.int32),
            pltpu.SMEM((tiles * pair,), jnp.int32),
            pltpu.SemaphoreType.DMA((2 + tiles,)),
        ]

    moved, kept = pl.pallas_call(
        functools.partial(stage_kernel, 0, tiles, pair),
        out_shape=[all_coded, jax.ShapeDtypeStruct(fronts.shape[2:], jnp.float32)],
        in_specs=[SMEM] * tiles + [ANY] * 3 + [VMEM] * 2 + [ANY] * tiles + [VMEM],
        out_specs=[VMEM] * 2,
        scratch_shapes=scratch(),
        name="first",
    )(*metas, object_slices, near, below, right3, left3, *brought, probe_wave)
    arrived = lax.ppermute(moved, "depth", [(d, d + 2) for d in range(0, depths - STEPS + 1, 2)])
    outs = pl.pallas_call(
        functools.partial(stage_kernel, 1, tiles, pair),
        out_shape=[coded] * tiles,
        in_specs=[SMEM] * tiles + [ANY] * 3 + [VMEM] * 2 + [ANY, VMEM, VMEM],
        out_specs=[VMEM] * tiles,
        scratch_shapes=scratch(),
        name="second",
    )(*metas, object_slices, near, above, right3, left3, arrived, kept, probe_wave)
    back = [
        lax.ppermute(
            outs[k], both, [(flat(d, t), flat(d + 1, t - k)) for d in range(depths) for t in range(tiles)]
        )
        for k in range(tiles)
    ]
    exits = pl.pallas_call(
        functools.partial(unpack_kernel, tiles, pair),
        out_shape=jax.ShapeDtypeStruct(fronts.shape[2:], jnp.float32),
        in_specs=[SMEM] + [VMEM] * tiles,
        out_specs=VMEM,
        name="unpack",
    )(meta, *back)
    return exits[None, None]


def solution(mesh):
    in_specs = (
        P("depth", "tile", None, None, None, None),
        P(),
        P("depth", None, "tile", None),
        P(None, "tile", None, None),
        P(None, "tile"),
    )
    out_specs = P("depth", "tile", None, None, None, None)
    return jax.shard_map(per_device, mesh=mesh, in_specs=in_specs, out_specs=out_specs, check_vma=False)
```

```python
import functools
import math

import jax
import jax.numpy as jnp
import ml_dtypes
import numpy as np
from jax import lax
from jax.experimental import pallas as pl
from jax.experimental.pallas import tpu as pltpu
from jax.sharding import PartitionSpec as P


STEPS = 4
FRESNEL_RATE = 0.3
EXTRA = 16
PLACES = 4
SPAN = 16
GROUP = 4

HBM = pl.BlockSpec(memory_space=pltpu.MemorySpace.HBM)
VMEM = pl.BlockSpec(memory_space=pltpu.VMEM)
PARAMS = pltpu.CompilerParams(vmem_limit_bytes=24 * 2**20)
SMEM = pl.BlockSpec(memory_space=pltpu.SMEM)


def halves(table):
    high = table.astype(ml_dtypes.bfloat16)
    low = (table - high.astype(np.float64)).astype(ml_dtypes.bfloat16)
    return high, low


@functools.lru_cache(None)
def propagators(width):
    index = np.arange(width)
    angle = 2.0 * np.pi * ((index[:, None] * index[None, :]) % width) / width
    freq = np.where(index < width // 2, index, index - width).astype(np.float64)
    factor = np.exp(-2j * np.pi * FRESNEL_RATE / width * freq**2)
    step = (np.exp(1j * angle) / width) @ (factor[:, None] * np.exp(-1j * angle))
    right = np.block([[step.real, step.imag], [-step.imag, step.real]])
    right_high, right_low = halves(right)
    left_high, left_low = halves(right.T)
    right3 = np.concatenate([right_high, right_high, right_low], axis=0)
    left3 = np.concatenate([left_high, left_high, left_low], axis=1)
    return right3, left3


def split(value):
    high = value.astype(jnp.bfloat16)
    low = (value - high.astype(jnp.float32)).astype(jnp.bfloat16)
    return high, low


def encode(real, imag, store):
    width = real.shape[0]
    codes = []
    for plane, value in enumerate((real, imag)):
        top = jnp.maximum(jnp.max(jnp.abs(value), axis=0, keepdims=True), 2.0**-100)
        code = jnp.ceil((jnp.log(top * (1.0 / 32766.0)) * (256.0 / math.log(2.0))))
        store(plane * width, jnp.round(value * jnp.exp2(code * (-1.0 / 256.0))).astype(jnp.int32).astype(jnp.int16))
        codes.append(code)
    return codes


def extra_rows(codes, places):
    width = codes[0].shape[1]
    rows = [
        jnp.broadcast_to(codes[0], (PLACES, width)),
        jnp.broadcast_to(places, (EXTRA // 2 - PLACES, width)),
        jnp.broadcast_to(codes[1], (EXTRA // 2, width)),
    ]
    return jnp.concatenate(rows, axis=0).astype(jnp.int32).astype(jnp.int16)


def decode(load, width):
    scales = jnp.exp2(load(2 * width, EXTRA).astype(jnp.int32).astype(jnp.float32) * (1.0 / 256.0))
    real = load(0, width).astype(jnp.int32).astype(jnp.float32) * scales[0:1]
    imag = load(width, width).astype(jnp.int32).astype(jnp.float32) * scales[EXTRA // 2 : EXTRA // 2 + 1]
    return real, imag


def nth_of_tile(tile_of, count, slots, tile, nth):
    found = jnp.int32(-1)
    seen = jnp.int32(0)
    for p in range(slots):
        hit = (tile_of(p) == tile) & (p < count)
        found = jnp.where(hit & (seen == nth), p, found)
        seen = seen + hit.astype(jnp.int32)
    return found


def batches():
    depth, depths = lax.axis_index("depth"), lax.axis_size("depth")
    return depths + STEPS - 2 - lax.rem(depth + STEPS - 1, depths), depths + STEPS - 2 - depth


def pack_kernel(tiles, pair, list_ref, count_ref, fronts_ref, slab_ref, right_ref, left_ref, *refs):
    out_refs = refs[:tiles]
    kept_refs = refs[tiles : tiles + 3]
    front_ref, in_sems, keep_sems = refs[tiles + 3 :]
    slots, _, width, _ = fronts_ref.shape
    own = lax.axis_index("tile")
    starting = batches()[0]

    def fetch(p):
        return pltpu.make_async_copy(fronts_ref.at[p], front_ref.at[p], in_sems.at[p])

    keeps = [
        pltpu.make_async_copy(source, target, keep_sems.at[n])
        for n, (source, target) in enumerate(zip((slab_ref, right_ref, left_ref), kept_refs))
    ]
    for p in range(slots):
        pl.when(p < count_ref[0, starting])(lambda p=p: fetch(p).start())
    for copy in keeps:
        copy.start()
    chosen = {}
    for k in range(tiles):
        tile = lax.rem(own + k, tiles)
        for i in range(pair):
            for b, batch in enumerate(batches()):
                chosen[k, i, b] = nth_of_tile(
                    lambda p: list_ref[0, 0, p, batch], count_ref[0, batch], slots, tile, i
                )
    for p in range(slots):
        pl.when(p < count_ref[0, starting])(lambda p=p: fetch(p).wait())
    lane = lax.broadcasted_iota(jnp.int32, (1, width), 1)
    for k in list(range(1, tiles)) + [0]:
        for i in range(pair):
            places = jnp.zeros((1, width), jnp.int32)
            for b, batch in enumerate(batches()):
                p = chosen[k, i, b]
                live = (p >= 0).astype(jnp.int32)
                at = jnp.maximum(p, 0)
                values = (live, list_ref[0, 1, at, batch], list_ref[0, 2, at, batch])
                for offset, value in enumerate(values):
                    places = jnp.where(lane == 3 * b + offset, value, places)
            places = places.astype(jnp.float32)
            p = chosen[k, i, 0]

            def store(row, block):
                out_refs[k][i, row : row + block.shape[0], :] = block

            @pl.when(p >= 0)
            def _():
                store(2 * width, extra_rows(encode(front_ref[p, 0], front_ref[p, 1], store), places))

            @pl.when(p < 0)
            def _():
                none = jnp.zeros((1, width), jnp.float32)
                store(2 * width, extra_rows((none, none), places))

    for copy in keeps:
        copy.wait()


def unpack_kernel(tiles, pair, list_ref, count_ref, *refs):
    in_refs, out_ref = refs[:tiles], refs[tiles]
    exit_ref, out_sems = refs[tiles + 1 :]
    slots, _, width, _ = out_ref.shape
    own = lax.axis_index("tile")
    batch = batches()[1]
    count = count_ref[0, batch]

    def send(p):
        return pltpu.make_async_copy(exit_ref.at[p], out_ref.at[p], out_sems.at[p])

    for p in range(slots):

        @pl.when(p >= count)
        def _():
            exit_ref[p] = jnp.zeros(exit_ref.shape[1:], jnp.float32)
            send(p).start()

    for k in range(tiles):
        tile = lax.rem(own + k, tiles)
        for i in range(pair):
            p = nth_of_tile(lambda p: list_ref[0, 0, p, batch], count, slots, tile, i)

            @pl.when(p >= 0)
            def _():
                real, imag = decode(lambda row, size: in_refs[k][i, row : row + size, :], width)
                exit_ref[p, 0] = real
                exit_ref[p, 1] = imag
                send(p).start()

    for p in range(slots):
        send(p).wait()


def cut(slab_ref, layer, row, column, patch_ref):
    width, side = patch_ref.shape[-1], slab_ref.shape[-1]
    block = jnp.minimum(column // width, side // width - 2)
    shift = column - block * width
    start = pl.multiple_of(row - row_offset(row, width, side), SPAN)
    rows = width + SPAN
    lane = lax.broadcasted_iota(jnp.int32, (rows, width), 1)
    turn = lax.rem(width - shift, width)
    for plane in range(2):
        parts = []
        for b in range(2):
            lanes = pl.ds(pl.multiple_of((block + b) * width, width), width)
            part = pltpu.roll(slab_ref[layer, plane, pl.ds(start, rows), lanes], turn, 1)
            parts.append(part.astype(jnp.float32))
        patch_ref[plane] = jnp.where(lane < width - shift, parts[0], parts[1])


def row_offset(row, width, side):
    return row - jnp.minimum((row // SPAN) * SPAN, side - width - SPAN)


def run_layers(steps, places, wave_ref, patch_ref, x_ref, y_ref, right_ref, left_ref):
    width = wave_ref.shape[1] // 2
    side = steps[0][0].shape[-1]

    def fill(which, turn):
        slab_ref, layer, _ = steps[which]
        for w in range(GROUP):
            cut(slab_ref, layer, *places[w], patch_ref.at[turn, w])

    def one(which):
        turn = which % 2
        for w in range(GROUP):
            rows = slice(w * width, (w + 1) * width)
            part = pl.ds(row_offset(places[w][0], width, side), width)
            real, imag = wave_ref[rows, :width], wave_ref[rows, width:]
            trans_real, trans_imag = patch_ref[turn, w, 0, part, :], patch_ref[turn, w, 1, part, :]
            for plane, value in enumerate((real * trans_real - imag * trans_imag, real * trans_imag + imag * trans_real)):
                high, low = split(value)
                x_ref[rows, plane * width : (plane + 1) * width] = high
                x_ref[rows, (2 + plane) * width : (3 + plane) * width] = low
                x_ref[rows, (4 + plane) * width : (5 + plane) * width] = high
        if which + 1 < len(steps):
            fill(which + 1, 1 - turn)
        spread = jnp.dot(x_ref[...], right_ref[...], preferred_element_type=jnp.float32)
        for w in range(GROUP):
            side_lanes = slice((w % 2) * width, (w % 2 + 1) * width)
            for plane in range(2):
                high, low = split(spread[w * width : (w + 1) * width, plane * width : (plane + 1) * width])
                y_ref[w // 2, plane * width : (plane + 1) * width, side_lanes] = high
                y_ref[w // 2, (2 + plane) * width : (3 + plane) * width, side_lanes] = low
                y_ref[w // 2, (4 + plane) * width : (5 + plane) * width, side_lanes] = high
        for g in range(GROUP // 2):
            out = jnp.dot(left_ref[...], y_ref[g], preferred_element_type=jnp.float32)
            for w in range(2):
                rows = slice((2 * g + w) * width, (2 * g + w + 1) * width)
                side_lanes = slice(w * width, (w + 1) * width)
                wave_ref[rows, :width] = out[:width, side_lanes]
                wave_ref[rows, width:] = out[width:, side_lanes]

    which = 0
    while which < len(steps):
        condition = steps[which][2]
        block = [which]
        while block[-1] + 1 < len(steps) and steps[block[-1] + 1][2] is condition:
            block.append(block[-1] + 1)

        def run(block=tuple(block)):
            if block[0] == 0:
                fill(0, 0)
            for step in block:
                one(step)

        if condition is None:
            run()
        else:
            pl.when(condition)(run)
            later = block[-1] + 1
            if later < len(steps):
                pl.when(jnp.logical_not(condition))(lambda later=later: fill(later, later % 2))
        which = block[-1] + 1


def read_places(in_refs, b, pair, column_ref, place_ref, sem):
    for n, ref in enumerate(in_refs):
        for i in range(pair):
            rows = ref[i, ref.shape[1] - EXTRA :, :].astype(jnp.int32)
            column_ref[n * pair + i : n * pair + i + 1, :] = rows[PLACES : PLACES + 1]
    copy = pltpu.make_async_copy(column_ref, place_ref, sem)
    copy.start()
    copy.wait()
    live, places = [], []
    for j in range(len(in_refs) * pair):
        on = place_ref[j, 3 * b]
        live.append(on == 1)
        places.append((place_ref[j, 3 * b + 1] * on, place_ref[j, 3 * b + 2] * on))
    return live, places


def wave_to(ref, j, width, real, imag):
    rows = slice(j * width, (j + 1) * width)
    ref[rows, :width] = real
    ref[rows, width:] = imag


def send_wave(wave_ref, j, width, ref, at):
    rows = slice(j * width, (j + 1) * width)

    def store(row, block):
        ref[at, row : row + block.shape[0], :] = block

    codes = encode(wave_ref[rows, :width], wave_ref[rows, width:], store)
    store(2 * width, extra_rows(codes, jnp.zeros((1, width), jnp.float32)))


def first_kernel(ks, pair, own_ref, next_ref, probe_ref, right_ref, left_ref, *refs):
    in_refs, move_ref = refs[: len(ks)], refs[len(ks)]
    column_ref, place_ref, sem, wave_ref, patch_ref, x_ref, y_ref = refs[len(ks) + 1 :]
    width = right_ref.shape[1] // 2
    depth, depths = lax.axis_index("depth"), lax.axis_size("depth")
    fresh = depth == depths - 1
    live, places = read_places(in_refs, 0, pair, column_ref, place_ref, sem)
    some = functools.reduce(jnp.logical_or, live)

    @pl.when(some & jnp.logical_or(fresh, depth + STEPS - 1 < depths))
    def _():
        for j in range(GROUP):
            source = in_refs[j // pair]

            @pl.when(fresh)
            def _():
                wave_to(wave_ref, j, width, probe_ref[0], probe_ref[1])

            @pl.when(jnp.logical_not(fresh))
            def _():
                wave_to(wave_ref, j, width, *decode(lambda row, size: source[j % pair, row : row + size, :], width))

        own = jnp.logical_not(fresh)
        steps = [(own_ref, 0, own), (own_ref, 1, own), (next_ref, 0, None), (next_ref, 1, None)]
        run_layers(steps, places, wave_ref, patch_ref, x_ref, y_ref, right_ref, left_ref)
        for j in range(GROUP):
            pl.when(live[j])(lambda j=j: send_wave(wave_ref, j, width, move_ref, j))


def second_kernel(ks, pair, last_ref, own_ref, probe_ref, right_ref, left_ref, arrived_ref, *refs):
    in_refs, out_refs = refs[: len(ks)], refs[len(ks) : 2 * len(ks)]
    column_ref, place_ref, sem, wave_ref, patch_ref, x_ref, y_ref = refs[2 * len(ks) :]
    width = right_ref.shape[1] // 2
    depth = lax.axis_index("depth")
    live, places = read_places(in_refs, 1, pair, column_ref, place_ref, sem)
    some = functools.reduce(jnp.logical_or, live)

    @pl.when(some)
    def _():
        fresh = depth < STEPS - 2
        for j in range(GROUP):

            @pl.when(fresh)
            def _():
                wave_to(wave_ref, j, width, probe_ref[0], probe_ref[1])

            @pl.when(jnp.logical_not(fresh))
            def _():
                wave_to(wave_ref, j, width, *decode(lambda row, size: arrived_ref[j, row : row + size, :], width))

        near = depth >= 1
        steps = [(last_ref, 0, near), (last_ref, 1, near), (own_ref, 0, None), (own_ref, 1, None)]
        run_layers(steps, places, wave_ref, patch_ref, x_ref, y_ref, right_ref, left_ref)
        for j in range(GROUP):
            pl.when(live[j])(lambda j=j: send_wave(wave_ref, j, width, out_refs[j // pair], j % pair))


def on_chip(value):
    return pltpu.with_memory_space_constraint(value, pltpu.MemorySpace.VMEM)


def off_chip(value):
    return pltpu.with_memory_space_constraint(value, pltpu.MemorySpace.HBM)


def per_device(fronts, probe_wave, object_slices, patch_list, counts):
    depths = lax.axis_size("depth")
    tiles = lax.axis_size("tile")
    slots = fronts.shape[2]
    width = fronts.shape[-1]
    pair = slots // tiles
    per_group = GROUP // pair
    groups = [tuple(range(g, g + per_group)) for g in range(0, tiles, per_group)]
    right3, left3 = (jnp.asarray(table) for table in propagators(width))
    coded_rows = 2 * width + EXTRA
    coded = pltpu.VMEM((pair, coded_rows, width), jnp.int16)
    lists = [jnp.transpose(patch_list, (1, 2, 3, 0)), jnp.transpose(counts)]
    lists = [off_chip(value) for value in lists]

    next_slab = on_chip(lax.ppermute(object_slices, "depth", [((d + 1) % depths, d) for d in range(depths)]))
    last_slab = on_chip(lax.ppermute(object_slices, "depth", [(d, d + 1) for d in range(depths - 1)]))
    *packed, own_slab, right, left = pl.pallas_call(
        functools.partial(pack_kernel, tiles, pair),
        out_shape=[coded] * tiles + [pltpu.VMEM(value.shape, value.dtype) for value in (object_slices, right3, left3)],
        in_specs=[SMEM, SMEM, HBM, HBM, HBM, HBM],
        out_specs=[VMEM] * (tiles + 3),
        scratch_shapes=[
            pltpu.VMEM(fronts.shape[2:], jnp.float32),
            pltpu.SemaphoreType.DMA((slots,)),
            pltpu.SemaphoreType.DMA((3,)),
        ],
        compiler_params=PARAMS,
        name="pack",
    )(*lists, *[off_chip(value) for value in (fronts[0, 0], object_slices, right3, left3)])

    def turned(k):
        return [(t, (t + k) % tiles) for t in range(tiles)]

    brought = [packed[0]]
    for k in range(1, tiles):
        brought.append(on_chip(lax.ppermute(packed[k], "tile", turned(k))))
    scratch = [
        pltpu.VMEM((8, width), jnp.int32),
        pltpu.SMEM((8, width), jnp.int32),
        pltpu.SemaphoreType.DMA,
        pltpu.VMEM((GROUP * width, 2 * width), jnp.float32),
        pltpu.VMEM((2, GROUP, 2, width + SPAN, width), jnp.float32),
        pltpu.VMEM((GROUP * width, 6 * width), jnp.bfloat16),
        pltpu.VMEM((GROUP // 2, 6 * width, 2 * width), jnp.bfloat16),
    ]
    moved_shape = pltpu.VMEM((GROUP, coded_rows, width), jnp.int16)
    flops = 2 * GROUP * (2 * 3) * width * (2 * width) ** 2
    arrived = []
    for ks in groups:
        moved = pl.pallas_call(
            functools.partial(first_kernel, ks, pair),
            out_shape=moved_shape,
            in_specs=[VMEM] * (5 + per_group),
            out_specs=VMEM,
            scratch_shapes=scratch,
            cost_estimate=pl.CostEstimate(flops=4 * flops, bytes_accessed=0, transcendentals=0),
            compiler_params=PARAMS,
        )(own_slab, next_slab, probe_wave, right, left, *[brought[k] for k in ks])
        pairs = [(d, d + STEPS - 1) for d in range(depths - STEPS + 1)] + [(depths - 1, STEPS - 2)]
        arrived.append(on_chip(lax.ppermute(moved, "depth", pairs)))
    back = [None] * tiles
    for g, ks in enumerate(groups):
        outs = pl.pallas_call(
            functools.partial(second_kernel, ks, pair),
            out_shape=[coded] * per_group,
            in_specs=[VMEM] * (6 + per_group),
            out_specs=[VMEM] * per_group,
            scratch_shapes=scratch,
            cost_estimate=pl.CostEstimate(flops=4 * flops, bytes_accessed=0, transcendentals=0),
            compiler_params=PARAMS,
        )(last_slab, own_slab, probe_wave, right, left, arrived[g], *[brought[k] for k in ks])
        for k, value in zip(ks, outs):
            if k == 0:
                back[k] = value
            else:
                back[k] = on_chip(lax.ppermute(value, "tile", turned(-k)))
    exits = pl.pallas_call(
        functools.partial(unpack_kernel, tiles, pair),
        out_shape=jax.ShapeDtypeStruct(fronts.shape[2:], jnp.float32),
        in_specs=[SMEM, SMEM] + [VMEM] * tiles,
        out_specs=HBM,
        scratch_shapes=[pltpu.VMEM(fronts.shape[2:], jnp.float32), pltpu.SemaphoreType.DMA((slots,))],
        compiler_params=PARAMS,
        name="unpack",
    )(*lists, *back)
    return exits[None, None]


def solution(mesh):
    in_specs = (
        P("depth", "tile", None, None, None, None),
        P(),
        P("depth", None, "tile", None),
        P(None, "tile", None, None),
        P(None, "tile"),
    )
    out_specs = P("depth", "tile", None, None, None, None)

    return jax.shard_map(per_device, mesh=mesh, in_specs=in_specs, out_specs=out_specs, check_vma=False)
```

```python
import functools
import math

import jax
import jax.numpy as jnp
import ml_dtypes
import numpy as np
from jax import lax
from jax.experimental import pallas as pl
from jax.experimental.pallas import tpu as pltpu
from jax.sharding import PartitionSpec as P


STEPS = 4
FRESNEL_RATE = 0.3
EXTRA = 16
PLACES = 4
SPAN = 16
GROUP = 4

HBM = pl.BlockSpec(memory_space=pltpu.MemorySpace.HBM)
VMEM = pl.BlockSpec(memory_space=pltpu.VMEM)
PARAMS = pltpu.CompilerParams(vmem_limit_bytes=24 * 2**20)
SMEM = pl.BlockSpec(memory_space=pltpu.SMEM)


def halves(table):
    high = table.astype(ml_dtypes.bfloat16)
    low = (table - high.astype(np.float64)).astype(ml_dtypes.bfloat16)
    return high, low


@functools.lru_cache(None)
def propagators(width):
    index = np.arange(width)
    angle = 2.0 * np.pi * ((index[:, None] * index[None, :]) % width) / width
    freq = np.where(index < width // 2, index, index - width).astype(np.float64)
    factor = np.exp(-2j * np.pi * FRESNEL_RATE / width * freq**2)
    step = (np.exp(1j * angle) / width) @ (factor[:, None] * np.exp(-1j * angle))
    right = np.block([[step.real, step.imag], [-step.imag, step.real]])
    right_high, right_low = halves(right)
    left_high, left_low = halves(right.T)
    right3 = np.concatenate([right_high, right_high, right_low], axis=0)
    left3 = np.concatenate([left_high, left_high, left_low], axis=1)
    return right3, left3


def split(value):
    high = value.astype(jnp.bfloat16)
    low = (value - high.astype(jnp.float32)).astype(jnp.bfloat16)
    return high, low


def encode(real, imag, store):
    width = real.shape[0]
    codes = []
    for plane, value in enumerate((real, imag)):
        top = jnp.maximum(jnp.max(jnp.abs(value), axis=0, keepdims=True), 2.0**-100)
        code = jnp.ceil((jnp.log(top * (1.0 / 32766.0)) * (256.0 / math.log(2.0))))
        store(plane * width, jnp.round(value * jnp.exp2(code * (-1.0 / 256.0))).astype(jnp.int32).astype(jnp.int16))
        codes.append(code)
    return codes


def extra_rows(codes, places):
    width = codes[0].shape[1]
    rows = [
        jnp.broadcast_to(codes[0], (PLACES, width)),
        jnp.broadcast_to(places, (EXTRA // 2 - PLACES, width)),
        jnp.broadcast_to(codes[1], (EXTRA // 2, width)),
    ]
    return jnp.concatenate(rows, axis=0).astype(jnp.int32).astype(jnp.int16)


def decode(load, width):
    scales = jnp.exp2(load(2 * width, EXTRA).astype(jnp.int32).astype(jnp.float32) * (1.0 / 256.0))
    real = load(0, width).astype(jnp.int32).astype(jnp.float32) * scales[0:1]
    imag = load(width, width).astype(jnp.int32).astype(jnp.float32) * scales[EXTRA // 2 : EXTRA // 2 + 1]
    return real, imag


def nth_of_tile(tile_of, count, slots, tile, nth):
    found = jnp.int32(-1)
    seen = jnp.int32(0)
    for p in range(slots):
        hit = (tile_of(p) == tile) & (p < count)
        found = jnp.where(hit & (seen == nth), p, found)
        seen = seen + hit.astype(jnp.int32)
    return found


def batches():
    depth, depths = lax.axis_index("depth"), lax.axis_size("depth")
    return depths + STEPS - 2 - lax.rem(depth + STEPS - 1, depths), depths + STEPS - 2 - depth


def prep_kernel(slab_ref, right_ref, left_ref, probe_ref, *refs):
    copies = [
        pltpu.make_async_copy(source, target, refs[4].at[n])
        for n, (source, target) in enumerate(zip((slab_ref, right_ref, left_ref, probe_ref), refs[:4]))
    ]
    for copy in copies:
        copy.start()
    for copy in copies:
        copy.wait()


def pack_kernel(tiles, pair, list_ref, count_ref, fronts_ref, *refs):
    out_refs = refs[:tiles]
    front_ref, in_sems = refs[tiles:]
    slots, _, width, _ = fronts_ref.shape
    own = lax.axis_index("tile")
    starting = batches()[0]

    def fetch(p):
        return pltpu.make_async_copy(fronts_ref.at[p], front_ref.at[p], in_sems.at[p])

    for p in range(slots):
        pl.when(p < count_ref[0, starting])(lambda p=p: fetch(p).start())
    chosen = {}
    for k in range(tiles):
        tile = lax.rem(own + k, tiles)
        for i in range(pair):
            for b, batch in enumerate(batches()):
                chosen[k, i, b] = nth_of_tile(
                    lambda p: list_ref[0, 0, p, batch], count_ref[0, batch], slots, tile, i
                )
    for p in range(slots):
        pl.when(p < count_ref[0, starting])(lambda p=p: fetch(p).wait())
    lane = lax.broadcasted_iota(jnp.int32, (1, width), 1)
    for k in list(range(1, tiles)) + [0]:
        for i in range(pair):
            places = jnp.zeros((1, width), jnp.int32)
            for b, batch in enumerate(batches()):
                p = chosen[k, i, b]
                live = (p >= 0).astype(jnp.int32)
                at = jnp.maximum(p, 0)
                values = (live, list_ref[0, 1, at, batch], list_ref[0, 2, at, batch])
                for offset, value in enumerate(values):
                    places = jnp.where(lane == 3 * b + offset, value, places)
            places = places.astype(jnp.float32)
            p = chosen[k, i, 0]

            def store(row, block):
                out_refs[k][i, row : row + block.shape[0], :] = block

            @pl.when(p >= 0)
            def _():
                store(2 * width, extra_rows(encode(front_ref[p, 0], front_ref[p, 1], store), places))

            @pl.when(p < 0)
            def _():
                none = jnp.zeros((1, width), jnp.float32)
                store(2 * width, extra_rows((none, none), places))


def unpack_kernel(tiles, pair, list_ref, count_ref, *refs):
    in_refs, out_ref = refs[:tiles], refs[tiles]
    exit_ref, out_sems = refs[tiles + 1 :]
    slots, _, width, _ = out_ref.shape
    own = lax.axis_index("tile")
    batch = batches()[1]
    count = count_ref[0, batch]

    def send(p):
        return pltpu.make_async_copy(exit_ref.at[p], out_ref.at[p], out_sems.at[p])

    for p in range(slots):

        @pl.when(p >= count)
        def _():
            exit_ref[p] = jnp.zeros(exit_ref.shape[1:], jnp.float32)
            send(p).start()

    for k in range(tiles):
        tile = lax.rem(own + k, tiles)
        for i in range(pair):
            p = nth_of_tile(lambda p: list_ref[0, 0, p, batch], count, slots, tile, i)

            @pl.when(p >= 0)
            def _():
                real, imag = decode(lambda row, size: in_refs[k][i, row : row + size, :], width)
                exit_ref[p, 0] = real
                exit_ref[p, 1] = imag
                send(p).start()

    for p in range(slots):
        send(p).wait()


def cut(slab_ref, layer, row, column, patch_ref):
    width, side = patch_ref.shape[-1], slab_ref.shape[-1]
    block = jnp.minimum(column // width, side // width - 2)
    shift = column - block * width
    start = pl.multiple_of(row - row_offset(row, width, side), SPAN)
    rows = width + SPAN
    lane = lax.broadcasted_iota(jnp.int32, (rows, width), 1)
    turn = lax.rem(width - shift, width)
    for plane in range(2):
        parts = []
        for b in range(2):
            lanes = pl.ds(pl.multiple_of((block + b) * width, width), width)
            part = pltpu.roll(slab_ref[layer, plane, pl.ds(start, rows), lanes], turn, 1)
            parts.append(part.astype(jnp.float32))
        patch_ref[plane] = jnp.where(lane < width - shift, parts[0], parts[1])


def row_offset(row, width, side):
    return row - jnp.minimum((row // SPAN) * SPAN, side - width - SPAN)


def run_layers(steps, places, wave_ref, patch_ref, x_refs, y_refs, right_ref, left_ref):
    width = wave_ref.shape[1] // 2
    side = steps[0][0].shape[-1]

    def fill(which, turn, pair):
        slab_ref, layer, _ = steps[which]
        for w in (2 * pair, 2 * pair + 1):
            cut(slab_ref, layer, *places[w], patch_ref.at[turn, w])

    def multiply(which, pair):
        turn = which % 2
        for n in range(2):
            w = 2 * pair + n
            rows = slice(w * width, (w + 1) * width)
            part = pl.ds(row_offset(places[w][0], width, side), width)
            real, imag = wave_ref[rows, :width], wave_ref[rows, width:]
            trans_real, trans_imag = patch_ref[turn, w, 0, part, :], patch_ref[turn, w, 1, part, :]
            rows = slice(n * width, (n + 1) * width)
            for plane, value in enumerate((real * trans_real - imag * trans_imag, real * trans_imag + imag * trans_real)):
                high, low = split(value)
                x_refs[pair][rows, plane * width : (plane + 1) * width] = high
                x_refs[pair][rows, (2 + plane) * width : (3 + plane) * width] = low

    def right(pair):
        x = x_refs[pair][...]
        x = jnp.concatenate([x, x[:, : 2 * width]], axis=1)
        spread = jnp.dot(x, right_ref[...], preferred_element_type=jnp.float32)
        for n in range(2):
            lanes = slice(n * width, (n + 1) * width)
            for plane in range(2):
                high, low = split(spread[n * width : (n + 1) * width, plane * width : (plane + 1) * width])
                y_refs[pair][plane * width : (plane + 1) * width, lanes] = high
                y_refs[pair][(2 + plane) * width : (3 + plane) * width, lanes] = low

    def left(pair):
        y = y_refs[pair][...]
        y = jnp.concatenate([y, y[: 2 * width]], axis=0)
        out = jnp.dot(left_ref[...], y, preferred_element_type=jnp.float32)
        for n in range(2):
            w = 2 * pair + n
            rows = slice(w * width, (w + 1) * width)
            lanes = slice(n * width, (n + 1) * width)
            wave_ref[rows, :width] = out[:width, lanes]
            wave_ref[rows, width:] = out[width:, lanes]

    def one(which):
        for pair in range(GROUP // 2):
            multiply(which, pair)
        for pair in range(GROUP // 2):
            right(pair)
            if which + 1 < len(steps):
                fill(which + 1, 1 - which % 2, pair)
        for pair in range(GROUP // 2):
            left(pair)

    which = 0
    while which < len(steps):
        condition = steps[which][2]
        block = [which]
        while block[-1] + 1 < len(steps) and steps[block[-1] + 1][2] is condition:
            block.append(block[-1] + 1)

        def run(block=tuple(block)):
            if block[0] == 0:
                for pair in range(GROUP // 2):
                    fill(0, 0, pair)
            for step in block:
                one(step)

        if condition is None:
            run()
        else:
            pl.when(condition)(run)
            later = block[-1] + 1
            if later < len(steps):

                def skip(later=later):
                    for pair in range(GROUP // 2):
                        fill(later, later % 2, pair)

                pl.when(jnp.logical_not(condition))(skip)
        which = block[-1] + 1


def read_places(in_refs, b, pair, column_ref, place_ref, sem):
    for n, ref in enumerate(in_refs):
        for i in range(pair):
            rows = ref[i, ref.shape[1] - EXTRA :, :].astype(jnp.int32)
            column_ref[n * pair + i : n * pair + i + 1, :] = rows[PLACES : PLACES + 1]
    copy = pltpu.make_async_copy(column_ref, place_ref, sem)
    copy.start()
    copy.wait()
    live, places = [], []
    for j in range(len(in_refs) * pair):
        on = place_ref[j, 3 * b]
        live.append(on == 1)
        places.append((place_ref[j, 3 * b + 1] * on, place_ref[j, 3 * b + 2] * on))
    return live, places


def wave_to(ref, j, width, real, imag):
    rows = slice(j * width, (j + 1) * width)
    ref[rows, :width] = real
    ref[rows, width:] = imag


def send_wave(wave_ref, j, width, ref, at):
    rows = slice(j * width, (j + 1) * width)

    def store(row, block):
        ref[at, row : row + block.shape[0], :] = block

    codes = encode(wave_ref[rows, :width], wave_ref[rows, width:], store)
    store(2 * width, extra_rows(codes, jnp.zeros((1, width), jnp.float32)))


def first_kernel(ks, pair, own_ref, next_ref, probe_ref, right_ref, left_ref, *refs):
    in_refs, move_ref = refs[: len(ks)], refs[len(ks)]
    column_ref, place_ref, sem, wave_ref, patch_ref, *buffers = refs[len(ks) + 1 :]
    width = right_ref.shape[1] // 2
    depth, depths = lax.axis_index("depth"), lax.axis_size("depth")
    fresh = depth == depths - 1
    live, places = read_places(in_refs, 0, pair, column_ref, place_ref, sem)
    some = functools.reduce(jnp.logical_or, live)

    @pl.when(some & jnp.logical_or(fresh, depth + STEPS - 1 < depths))
    def _():
        for j in range(GROUP):
            source = in_refs[j // pair]

            @pl.when(fresh)
            def _():
                wave_to(wave_ref, j, width, probe_ref[0], probe_ref[1])

            @pl.when(jnp.logical_not(fresh))
            def _():
                wave_to(wave_ref, j, width, *decode(lambda row, size: source[j % pair, row : row + size, :], width))

        own = jnp.logical_not(fresh)
        steps = [(own_ref, 0, own), (own_ref, 1, own), (next_ref, 0, None), (next_ref, 1, None)]
        run_layers(steps, places, wave_ref, patch_ref, buffers[:2], buffers[2:], right_ref, left_ref)
        for j in range(GROUP):
            pl.when(live[j])(lambda j=j: send_wave(wave_ref, j, width, move_ref, j))


def second_kernel(ks, pair, last_ref, own_ref, probe_ref, right_ref, left_ref, arrived_ref, *refs):
    in_refs, out_refs = refs[: len(ks)], refs[len(ks) : 2 * len(ks)]
    column_ref, place_ref, sem, wave_ref, patch_ref, *buffers = refs[2 * len(ks) :]
    width = right_ref.shape[1] // 2
    depth = lax.axis_index("depth")
    live, places = read_places(in_refs, 1, pair, column_ref, place_ref, sem)
    some = functools.reduce(jnp.logical_or, live)

    @pl.when(some)
    def _():
        fresh = depth < STEPS - 2
        for j in range(GROUP):

            @pl.when(fresh)
            def _():
                wave_to(wave_ref, j, width, probe_ref[0], probe_ref[1])

            @pl.when(jnp.logical_not(fresh))
            def _():
                wave_to(wave_ref, j, width, *decode(lambda row, size: arrived_ref[j, row : row + size, :], width))

        near = depth >= 1
        steps = [(last_ref, 0, near), (last_ref, 1, near), (own_ref, 0, None), (own_ref, 1, None)]
        run_layers(steps, places, wave_ref, patch_ref, buffers[:2], buffers[2:], right_ref, left_ref)
        for j in range(GROUP):
            pl.when(live[j])(lambda j=j: send_wave(wave_ref, j, width, out_refs[j // pair], j % pair))


def on_chip(value):
    return pltpu.with_memory_space_constraint(value, pltpu.MemorySpace.VMEM)


def off_chip(value):
    return pltpu.with_memory_space_constraint(value, pltpu.MemorySpace.HBM)


def per_device(fronts, probe_wave, object_slices, patch_list, counts):
    depths = lax.axis_size("depth")
    tiles = lax.axis_size("tile")
    slots = fronts.shape[2]
    width = fronts.shape[-1]
    pair = slots // tiles
    per_group = GROUP // pair
    groups = [tuple(range(g, g + per_group)) for g in range(0, tiles, per_group)][::-1]
    right3, left3 = (jnp.asarray(table) for table in propagators(width))
    coded_rows = 2 * width + EXTRA
    coded = pltpu.VMEM((pair, coded_rows, width), jnp.int16)
    lists = [jnp.transpose(patch_list, (1, 2, 3, 0)), jnp.transpose(counts)]
    lists = [off_chip(value) for value in lists]

    next_slab = on_chip(lax.ppermute(object_slices, "depth", [((d + 1) % depths, d) for d in range(depths)]))
    last_slab = on_chip(lax.ppermute(object_slices, "depth", [(d, d + 1) for d in range(depths - 1)]))
    packed = pl.pallas_call(
        functools.partial(pack_kernel, tiles, pair),
        out_shape=[coded] * tiles,
        in_specs=[SMEM, SMEM, HBM],
        out_specs=[VMEM] * tiles,
        scratch_shapes=[pltpu.VMEM(fronts.shape[2:], jnp.float32), pltpu.SemaphoreType.DMA((slots,))],
        compiler_params=PARAMS,
        name="pack",
    )(*lists, off_chip(fronts[0, 0]))
    kept = (object_slices, right3, left3, probe_wave)
    own_slab, right, left, probe = pl.pallas_call(
        prep_kernel,
        out_shape=[pltpu.VMEM(value.shape, value.dtype) for value in kept],
        in_specs=[HBM] * 4,
        out_specs=[VMEM] * 4,
        scratch_shapes=[pltpu.SemaphoreType.DMA((4,))],
        compiler_params=PARAMS,
        name="prep",
    )(*[off_chip(value) for value in kept])

    def turned(k):
        return [(t, (t + k) % tiles) for t in range(tiles)]

    brought = [packed[0]]
    for k in range(1, tiles):
        brought.append(on_chip(lax.ppermute(packed[k], "tile", turned(k))))
    scratch = [
        pltpu.VMEM((8, width), jnp.int32),
        pltpu.SMEM((8, width), jnp.int32),
        pltpu.SemaphoreType.DMA,
        pltpu.VMEM((GROUP * width, 2 * width), jnp.float32),
        pltpu.VMEM((2, GROUP, 2, width + SPAN, width), jnp.float32),
        *[pltpu.VMEM((2 * width, 4 * width), jnp.bfloat16)] * (GROUP // 2),
        *[pltpu.VMEM((4 * width, 2 * width), jnp.bfloat16)] * (GROUP // 2),
    ]
    moved_shape = pltpu.VMEM((GROUP, coded_rows, width), jnp.int16)
    flops = 2 * GROUP * (2 * 3) * width * (2 * width) ** 2
    arrived = []
    for ks in groups:
        moved = pl.pallas_call(
            functools.partial(first_kernel, ks, pair),
            out_shape=moved_shape,
            in_specs=[VMEM] * (5 + per_group),
            out_specs=VMEM,
            scratch_shapes=scratch,
            cost_estimate=pl.CostEstimate(flops=4 * flops, bytes_accessed=0, transcendentals=0),
            compiler_params=PARAMS,
        )(own_slab, next_slab, probe, right, left, *[brought[k] for k in ks])
        pairs = [(d, d + STEPS - 1) for d in range(depths - STEPS + 1)] + [(depths - 1, STEPS - 2)]
        arrived.append(on_chip(lax.ppermute(moved, "depth", pairs)))
    back = [None] * tiles
    for g, ks in enumerate(groups):
        outs = pl.pallas_call(
            functools.partial(second_kernel, ks, pair),
            out_shape=[coded] * per_group,
            in_specs=[VMEM] * (6 + per_group),
            out_specs=[VMEM] * per_group,
            scratch_shapes=scratch,
            cost_estimate=pl.CostEstimate(flops=4 * flops, bytes_accessed=0, transcendentals=0),
            compiler_params=PARAMS,
        )(last_slab, own_slab, probe, right, left, arrived[g], *[brought[k] for k in ks])
        for k, value in zip(ks, outs):
            if k == 0:
                back[k] = value
            else:
                back[k] = on_chip(lax.ppermute(value, "tile", turned(-k)))
    exits = pl.pallas_call(
        functools.partial(unpack_kernel, tiles, pair),
        out_shape=jax.ShapeDtypeStruct(fronts.shape[2:], jnp.float32),
        in_specs=[SMEM, SMEM] + [VMEM] * tiles,
        out_specs=HBM,
        scratch_shapes=[pltpu.VMEM(fronts.shape[2:], jnp.float32), pltpu.SemaphoreType.DMA((slots,))],
        compiler_params=PARAMS,
        name="unpack",
    )(*lists, *back)
    return exits[None, None]


def solution(mesh):
    in_specs = (
        P("depth", "tile", None, None, None, None),
        P(),
        P("depth", None, "tile", None),
        P(None, "tile", None, None),
        P(None, "tile"),
    )
    out_specs = P("depth", "tile", None, None, None, None)

    return jax.shard_map(per_device, mesh=mesh, in_specs=in_specs, out_specs=out_specs, check_vma=False)
```

```python
import functools
import math

import jax
import jax.numpy as jnp
import ml_dtypes
import numpy as np
from jax import lax
from jax.experimental import pallas as pl
from jax.experimental.pallas import tpu as pltpu
from jax.sharding import PartitionSpec as P


STEPS = 4
FRESNEL_RATE = 0.3
EXTRA = 16
PLACES = 4
SPAN = 16
ROWS = 16
GROUP = 4

HBM = pl.BlockSpec(memory_space=pltpu.MemorySpace.HBM)
VMEM = pl.BlockSpec(memory_space=pltpu.VMEM)
PARAMS = pltpu.CompilerParams(vmem_limit_bytes=24 * 2**20)
SMEM = pl.BlockSpec(memory_space=pltpu.SMEM)


def halves(table):
    high = table.astype(ml_dtypes.bfloat16)
    low = (table - high.astype(np.float64)).astype(ml_dtypes.bfloat16)
    return high, low


@functools.lru_cache(None)
def propagators(width):
    index = np.arange(width)
    angle = 2.0 * np.pi * ((index[:, None] * index[None, :]) % width) / width
    freq = np.where(index < width // 2, index, index - width).astype(np.float64)
    factor = np.exp(-2j * np.pi * FRESNEL_RATE / width * freq**2)
    step = (np.exp(1j * angle) / width) @ (factor[:, None] * np.exp(-1j * angle))
    right = np.block([[step.real, step.imag], [-step.imag, step.real]])
    right_high, right_low = halves(right)
    left_high, left_low = halves(right.T)
    right3 = np.concatenate([right_high, right_high, right_low], axis=0)
    left3 = np.concatenate([left_high, left_high, left_low], axis=1)
    left3 = left3.reshape(2, width // ROWS, ROWS, -1).swapaxes(0, 1).reshape(left3.shape)
    return right3, left3


def split(value):
    high = value.astype(jnp.bfloat16)
    low = (value - high.astype(jnp.float32)).astype(jnp.bfloat16)
    return high, low


def encode(real, imag, store):
    width = real.shape[0]
    codes = []
    for plane, value in enumerate((real, imag)):
        top = jnp.maximum(jnp.max(jnp.abs(value), axis=0, keepdims=True), 2.0**-100)
        code = jnp.ceil((jnp.log(top * (1.0 / 32766.0)) * (256.0 / math.log(2.0))))
        store(plane * width, jnp.round(value * jnp.exp2(code * (-1.0 / 256.0))).astype(jnp.int32).astype(jnp.int16))
        codes.append(code)
    return codes


def extra_rows(codes, places):
    width = codes[0].shape[1]
    rows = [
        jnp.broadcast_to(codes[0], (PLACES, width)),
        jnp.broadcast_to(places, (EXTRA // 2 - PLACES, width)),
        jnp.broadcast_to(codes[1], (EXTRA // 2, width)),
    ]
    return jnp.concatenate(rows, axis=0).astype(jnp.int32).astype(jnp.int16)


def decode(load, width):
    scales = jnp.exp2(load(2 * width, EXTRA).astype(jnp.int32).astype(jnp.float32) * (1.0 / 256.0))
    real = load(0, width).astype(jnp.int32).astype(jnp.float32) * scales[0:1]
    imag = load(width, width).astype(jnp.int32).astype(jnp.float32) * scales[EXTRA // 2 : EXTRA // 2 + 1]
    return real, imag


def nth_of_tile(tile_of, count, slots, tile, nth):
    found = jnp.int32(-1)
    seen = jnp.int32(0)
    for p in range(slots):
        hit = (tile_of(p) == tile) & (p < count)
        found = jnp.where(hit & (seen == nth), p, found)
        seen = seen + hit.astype(jnp.int32)
    return found


def batches():
    depth, depths = lax.axis_index("depth"), lax.axis_size("depth")
    latest = depths + STEPS - 2
    return latest - jnp.minimum(depth + STEPS - 1, depths - 1), latest - lax.rem(depth + 1, depths)


def prep_kernel(slab_ref, right_ref, left_ref, probe_ref, *refs):
    copies = [
        pltpu.make_async_copy(source, target, refs[4].at[n])
        for n, (source, target) in enumerate(zip((slab_ref, right_ref, left_ref, probe_ref), refs[:4]))
    ]
    for copy in copies:
        copy.start()
    for copy in copies:
        copy.wait()


def pack_kernel(tiles, pair, list_ref, count_ref, fronts_ref, *refs):
    out_refs = refs[:tiles]
    front_ref, in_sems = refs[tiles:]
    slots, _, width, _ = fronts_ref.shape
    own = lax.axis_index("tile")
    starting = batches()[0]

    def fetch(p):
        return pltpu.make_async_copy(fronts_ref.at[p], front_ref.at[p], in_sems.at[p])

    for p in range(slots):
        pl.when(p < count_ref[0, starting])(lambda p=p: fetch(p).start())
    chosen = {}
    for k in range(tiles):
        tile = lax.rem(own + k, tiles)
        for i in range(pair):
            for b, batch in enumerate(batches()):
                chosen[k, i, b] = nth_of_tile(
                    lambda p: list_ref[0, 0, p, batch], count_ref[0, batch], slots, tile, i
                )
    for p in range(slots):
        pl.when(p < count_ref[0, starting])(lambda p=p: fetch(p).wait())
    lane = lax.broadcasted_iota(jnp.int32, (1, width), 1)
    for k in list(range(1, tiles)) + [0]:
        for i in range(pair):
            places = jnp.zeros((1, width), jnp.int32)
            for b, batch in enumerate(batches()):
                p = chosen[k, i, b]
                live = (p >= 0).astype(jnp.int32)
                at = jnp.maximum(p, 0)
                values = (live, list_ref[0, 1, at, batch], list_ref[0, 2, at, batch])
                for offset, value in enumerate(values):
                    places = jnp.where(lane == 3 * b + offset, value, places)
            places = places.astype(jnp.float32)
            p = chosen[k, i, 0]

            def store(row, block):
                out_refs[k][i, row : row + block.shape[0], :] = block

            @pl.when(p >= 0)
            def _():
                store(2 * width, extra_rows(encode(front_ref[p, 0], front_ref[p, 1], store), places))

            @pl.when(p < 0)
            def _():
                none = jnp.zeros((1, width), jnp.float32)
                store(2 * width, extra_rows((none, none), places))


def unpack_kernel(tiles, pair, list_ref, count_ref, *refs):
    in_refs, out_ref = refs[:tiles], refs[tiles]
    exit_ref, out_sems = refs[tiles + 1 :]
    slots, _, width, _ = out_ref.shape
    own = lax.axis_index("tile")
    batch = lax.axis_size("depth") + STEPS - 2 - lax.axis_index("depth")
    count = count_ref[0, batch]

    def send(p):
        return pltpu.make_async_copy(exit_ref.at[p], out_ref.at[p], out_sems.at[p])

    for p in range(slots):

        @pl.when(p >= count)
        def _():
            exit_ref[p] = jnp.zeros(exit_ref.shape[1:], jnp.float32)
            send(p).start()

    for k in range(tiles):
        tile = lax.rem(own + k, tiles)
        for i in range(pair):
            p = nth_of_tile(lambda p: list_ref[0, 0, p, batch], count, slots, tile, i)

            @pl.when(p >= 0)
            def _():
                real, imag = decode(lambda row, size: in_refs[k][i, row : row + size, :], width)
                exit_ref[p, 0] = real
                exit_ref[p, 1] = imag
                send(p).start()

    for p in range(slots):
        send(p).wait()


def cut(slab_ref, layer, row, column, patch_ref):
    width, side = patch_ref.shape[-1], slab_ref.shape[-1]
    block = jnp.minimum(column // width, side // width - 2)
    shift = column - block * width
    start = pl.multiple_of(row - row_offset(row, width, side), SPAN)
    rows = width + SPAN
    lane = lax.broadcasted_iota(jnp.int32, (rows, width), 1)
    turn = lax.rem(width - shift, width)
    for plane in range(2):
        parts = []
        for b in range(2):
            lanes = pl.ds(pl.multiple_of((block + b) * width, width), width)
            parts.append(pltpu.roll(slab_ref[layer, plane, pl.ds(start, rows), lanes], turn, 1))
        patch_ref[plane] = jnp.where(lane < width - shift, parts[0], parts[1]).astype(jnp.float32)


def row_offset(row, width, side):
    return row - jnp.minimum((row // SPAN) * SPAN, side - width - SPAN)


def run_layers(steps, places, wave_ref, patch_ref, x_refs, y_refs, right_ref, left_ref):
    width = wave_ref.shape[1] // 2
    side = steps[0][0].shape[-1]

    def fill(which, turn, pair):
        slab_ref, layer, _ = steps[which]
        for w in (2 * pair, 2 * pair + 1):
            cut(slab_ref, layer, *places[w], patch_ref.at[turn, w])

    def multiply(which, pair, n, first_row, real, imag):
        turn = which % 2
        w = 2 * pair + n
        start = row_offset(places[w][0], width, side) + first_row
        part = pl.ds(start, real.shape[0])
        trans_real, trans_imag = patch_ref[turn, w, 0, part, :], patch_ref[turn, w, 1, part, :]
        rows = slice(n * width + first_row, n * width + first_row + real.shape[0])
        for plane, value in enumerate((real * trans_real - imag * trans_imag, real * trans_imag + imag * trans_real)):
            high, low = split(value)
            x_refs[pair][rows, plane * width : (plane + 1) * width] = high
            x_refs[pair][rows, (2 + plane) * width : (3 + plane) * width] = low

    def enter(which, pair):
        for n in range(2):
            rows = slice((2 * pair + n) * width, (2 * pair + n + 1) * width)
            multiply(which, pair, n, 0, wave_ref[rows, :width], wave_ref[rows, width:])

    def right(pair):
        spreads = []
        for n in range(2):
            x = x_refs[pair][n * width : (n + 1) * width]
            x = jnp.concatenate([x, x[:, : 2 * width]], axis=1)
            spreads.append(jnp.dot(x, right_ref[...], preferred_element_type=jnp.float32))
        for n, spread in enumerate(spreads):
            lanes = slice(n * width, (n + 1) * width)
            for b in range(width // ROWS):
                for plane in range(2):
                    rows = slice(b * ROWS, (b + 1) * ROWS)
                    high, low = split(spread[rows, plane * width : (plane + 1) * width])
                    start = plane * width + b * ROWS
                    y_refs[pair][start : start + ROWS, lanes] = high
                    y_refs[pair][2 * width + start : 2 * width + start + ROWS, lanes] = low

    def left(pair, ahead):
        y = y_refs[pair][...]
        y = jnp.concatenate([y, y[: 2 * width]], axis=0)
        outs = [
            jnp.dot(left_ref[half * width : (half + 1) * width], y, preferred_element_type=jnp.float32)
            for half in range(2)
        ]
        for b in range(width // ROWS):
            out, c = outs[2 * b // (width // ROWS)], b % (width // ROWS // 2)
            for n in range(2):
                lanes = slice(n * width, (n + 1) * width)
                real = out[2 * c * ROWS : (2 * c + 1) * ROWS, lanes]
                imag = out[(2 * c + 1) * ROWS : (2 * c + 2) * ROWS, lanes]
                if ahead is None:
                    rows = slice((2 * pair + n) * width + b * ROWS, (2 * pair + n) * width + (b + 1) * ROWS)
                    wave_ref[rows, :width] = real
                    wave_ref[rows, width:] = imag
                else:
                    multiply(ahead, pair, n, b * ROWS, real, imag)

    def one(which, ends):
        for pair in range(GROUP // 2):
            right(pair)
            if which + 1 < len(steps):
                fill(which + 1, 1 - which % 2, pair)
        for pair in range(GROUP // 2):
            left(pair, None if ends else which + 1)

    which = 0
    while which < len(steps):
        condition = steps[which][2]
        block = [which]
        while block[-1] + 1 < len(steps) and steps[block[-1] + 1][2] is condition:
            block.append(block[-1] + 1)

        def run(block=tuple(block)):
            if block[0] == 0:
                for pair in range(GROUP // 2):
                    fill(0, 0, pair)
            for pair in range(GROUP // 2):
                enter(block[0], pair)
            for step in block:
                one(step, step == block[-1])

        if condition is None:
            run()
        else:
            pl.when(condition)(run)
            later = block[-1] + 1
            if later < len(steps):

                def skip(later=later):
                    for pair in range(GROUP // 2):
                        fill(later, later % 2, pair)

                pl.when(jnp.logical_not(condition))(skip)
        which = block[-1] + 1


def read_places(in_refs, b, pair, column_ref, place_ref, sem):
    for n, ref in enumerate(in_refs):
        for i in range(pair):
            rows = ref[i, ref.shape[1] - EXTRA :, :].astype(jnp.int32)
            column_ref[n * pair + i : n * pair + i + 1, :] = rows[PLACES : PLACES + 1]
    copy = pltpu.make_async_copy(column_ref, place_ref, sem)
    copy.start()
    copy.wait()
    live, places = [], []
    for j in range(len(in_refs) * pair):
        on = place_ref[j, 3 * b]
        live.append(on == 1)
        places.append((place_ref[j, 3 * b + 1] * on, place_ref[j, 3 * b + 2] * on))
    return live, places


def wave_to(ref, j, width, real, imag):
    rows = slice(j * width, (j + 1) * width)
    ref[rows, :width] = real
    ref[rows, width:] = imag


def send_wave(wave_ref, j, width, ref, at):
    rows = slice(j * width, (j + 1) * width)

    def store(row, block):
        ref[at, row : row + block.shape[0], :] = block

    codes = encode(wave_ref[rows, :width], wave_ref[rows, width:], store)
    store(2 * width, extra_rows(codes, jnp.zeros((1, width), jnp.float32)))


def first_kernel(ks, pair, own_ref, next_ref, right_ref, left_ref, *refs):
    in_refs, move_ref = refs[: len(ks)], refs[len(ks)]
    column_ref, place_ref, sem, wave_ref, patch_ref, *buffers = refs[len(ks) + 1 :]
    width = right_ref.shape[1] // 2
    depth, depths = lax.axis_index("depth"), lax.axis_size("depth")
    live, places = read_places(in_refs, 0, pair, column_ref, place_ref, sem)
    some = functools.reduce(jnp.logical_or, live)

    @pl.when(some & (depth + STEPS - 1 < depths))
    def _():
        for j in range(GROUP):
            source = in_refs[j // pair]
            wave_to(wave_ref, j, width, *decode(lambda row, size: source[j % pair, row : row + size, :], width))
        even = lax.rem(depth, 2) == 0
        steps = [(own_ref, 0, None), (own_ref, 1, None), (next_ref, 0, even), (next_ref, 1, even)]
        run_layers(steps, places, wave_ref, patch_ref, buffers[:2], buffers[2:], right_ref, left_ref)
        for j in range(GROUP):
            pl.when(live[j])(lambda j=j: send_wave(wave_ref, j, width, move_ref, j))


def second_kernel(ks, pair, last_ref, own_ref, next_ref, probe_ref, right_ref, left_ref, arrived_ref, *refs):
    in_refs, out_refs = refs[: len(ks)], refs[len(ks) : 2 * len(ks)]
    column_ref, place_ref, sem, wave_ref, patch_ref, *buffers = refs[2 * len(ks) :]
    width = right_ref.shape[1] // 2
    depth, depths = lax.axis_index("depth"), lax.axis_size("depth")
    live, places = read_places(in_refs, 1, pair, column_ref, place_ref, sem)
    some = functools.reduce(jnp.logical_or, live)

    @pl.when(some)
    def _():
        final = depth == depths - 1
        fresh = jnp.logical_or(depth < 2, final)
        for j in range(GROUP):

            @pl.when(fresh)
            def _():
                wave_to(wave_ref, j, width, probe_ref[0], probe_ref[1])

            @pl.when(jnp.logical_not(fresh))
            def _():
                wave_to(wave_ref, j, width, *decode(lambda row, size: arrived_ref[j, row : row + size, :], width))

        inner = jnp.logical_not(final)
        below = inner & (lax.rem(depth, 2) == 1)
        steps = [(last_ref, 0, below), (last_ref, 1, below), (own_ref, 0, inner), (own_ref, 1, inner)]
        steps += [(next_ref, 0, None), (next_ref, 1, None)]
        run_layers(steps, places, wave_ref, patch_ref, buffers[:2], buffers[2:], right_ref, left_ref)
        for j in range(GROUP):
            pl.when(live[j])(lambda j=j: send_wave(wave_ref, j, width, out_refs[j // pair], j % pair))


def on_chip(value):
    return pltpu.with_memory_space_constraint(value, pltpu.MemorySpace.VMEM)


def off_chip(value):
    return pltpu.with_memory_space_constraint(value, pltpu.MemorySpace.HBM)


def per_device(fronts, probe_wave, object_slices, patch_list, counts):
    depths = lax.axis_size("depth")
    tiles = lax.axis_size("tile")
    slots = fronts.shape[2]
    width = fronts.shape[-1]
    pair = slots // tiles
    per_group = GROUP // pair
    groups = [tuple(range(g, g + per_group)) for g in range(0, tiles, per_group)][::-1]
    right3, left3 = (jnp.asarray(table) for table in propagators(width))
    coded_rows = 2 * width + EXTRA
    coded = pltpu.VMEM((pair, coded_rows, width), jnp.int16)
    lists = [jnp.transpose(patch_list, (1, 2, 3, 0)), jnp.transpose(counts)]
    lists = [off_chip(value) for value in lists]

    next_slab = on_chip(lax.ppermute(object_slices, "depth", [((d + 1) % depths, d) for d in range(depths)]))
    last_slab = on_chip(lax.ppermute(object_slices, "depth", [(d, d + 1) for d in range(0, depths, 2)]))
    packed = pl.pallas_call(
        functools.partial(pack_kernel, tiles, pair),
        out_shape=[coded] * tiles,
        in_specs=[SMEM, SMEM, HBM],
        out_specs=[VMEM] * tiles,
        scratch_shapes=[pltpu.VMEM(fronts.shape[2:], jnp.float32), pltpu.SemaphoreType.DMA((slots,))],
        compiler_params=PARAMS,
        name="pack",
    )(*lists, off_chip(fronts[0, 0]))
    kept = (object_slices, right3, left3, probe_wave)
    own_slab, right, left, probe = pl.pallas_call(
        prep_kernel,
        out_shape=[pltpu.VMEM(value.shape, value.dtype) for value in kept],
        in_specs=[HBM] * 4,
        out_specs=[VMEM] * 4,
        scratch_shapes=[pltpu.SemaphoreType.DMA((4,))],
        compiler_params=PARAMS,
        name="prep",
    )(*[off_chip(value) for value in kept])

    def flat(depth, tile):
        return (depth % depths) * tiles + tile % tiles

    def turned(k):
        return [(t, (t + k) % tiles) for t in range(tiles)]

    brought = [packed[0]]
    for k in range(1, tiles):
        brought.append(on_chip(lax.ppermute(packed[k], "tile", turned(k))))
    scratch = [
        pltpu.VMEM((8, width), jnp.int32),
        pltpu.SMEM((8, width), jnp.int32),
        pltpu.SemaphoreType.DMA,
        pltpu.VMEM((GROUP * width, 2 * width), jnp.float32),
        pltpu.VMEM((2, GROUP, 2, width + SPAN, width), jnp.float32),
        *[pltpu.VMEM((2 * width, 4 * width), jnp.bfloat16)] * (GROUP // 2),
        *[pltpu.VMEM((4 * width, 2 * width), jnp.bfloat16)] * (GROUP // 2),
    ]
    moved_shape = pltpu.VMEM((GROUP, coded_rows, width), jnp.int16)
    flops = 2 * GROUP * (2 * 3) * width * (2 * width) ** 2
    arrived = []
    for ks in groups:
        moved = pl.pallas_call(
            functools.partial(first_kernel, ks, pair),
            out_shape=moved_shape,
            in_specs=[VMEM] * (4 + per_group),
            out_specs=VMEM,
            scratch_shapes=scratch,
            cost_estimate=pl.CostEstimate(flops=4 * flops, bytes_accessed=0, transcendentals=0),
            compiler_params=PARAMS,
        )(own_slab, next_slab, right, left, *[brought[k] for k in ks])
        pairs = [(d, d + 2) for d in range(depths - STEPS + 1)]
        arrived.append(on_chip(lax.ppermute(moved, "depth", pairs)))
    back = [None] * tiles
    for g, ks in enumerate(groups):
        outs = pl.pallas_call(
            functools.partial(second_kernel, ks, pair),
            out_shape=[coded] * per_group,
            in_specs=[VMEM] * (7 + per_group),
            out_specs=[VMEM] * per_group,
            scratch_shapes=scratch,
            cost_estimate=pl.CostEstimate(flops=4 * flops, bytes_accessed=0, transcendentals=0),
            compiler_params=PARAMS,
        )(last_slab, own_slab, next_slab, probe, right, left, arrived[g], *[brought[k] for k in ks])
        for k, value in zip(ks, outs):
            pairs = [(flat(d, t), flat(d + 1, t - k)) for d in range(depths) for t in range(tiles)]
            back[k] = on_chip(lax.ppermute(value, ("depth", "tile"), pairs))
    exits = pl.pallas_call(
        functools.partial(unpack_kernel, tiles, pair),
        out_shape=jax.ShapeDtypeStruct(fronts.shape[2:], jnp.float32),
        in_specs=[SMEM, SMEM] + [VMEM] * tiles,
        out_specs=HBM,
        scratch_shapes=[pltpu.VMEM(fronts.shape[2:], jnp.float32), pltpu.SemaphoreType.DMA((slots,))],
        compiler_params=PARAMS,
        name="unpack",
    )(*lists, *back)
    return exits[None, None]


def solution(mesh):
    in_specs = (
        P("depth", "tile", None, None, None, None),
        P(),
        P("depth", None, "tile", None),
        P(None, "tile", None, None),
        P(None, "tile"),
    )
    out_specs = P("depth", "tile", None, None, None, None)

    return jax.shard_map(per_device, mesh=mesh, in_specs=in_specs, out_specs=out_specs, check_vma=False)
```

```python
import functools
import math

import jax
import jax.numpy as jnp
import ml_dtypes
import numpy as np
from jax import lax
from jax.experimental import pallas as pl
from jax.experimental.pallas import tpu as pltpu
from jax.sharding import PartitionSpec as P


STEPS = 4
FRESNEL_RATE = 0.3
EXTRA = 16
PLACES = 4
SPAN = 16
ROWS = 16
GROUP = 4

HBM = pl.BlockSpec(memory_space=pltpu.MemorySpace.HBM)
VMEM = pl.BlockSpec(memory_space=pltpu.VMEM)
PARAMS = pltpu.CompilerParams(vmem_limit_bytes=24 * 2**20)
SMEM = pl.BlockSpec(memory_space=pltpu.SMEM)


def halves(table):
    high = table.astype(ml_dtypes.bfloat16)
    low = (table - high.astype(np.float64)).astype(ml_dtypes.bfloat16)
    return high, low


@functools.lru_cache(None)
def propagators(width):
    index = np.arange(width)
    angle = 2.0 * np.pi * ((index[:, None] * index[None, :]) % width) / width
    freq = np.where(index < width // 2, index, index - width).astype(np.float64)
    factor = np.exp(-2j * np.pi * FRESNEL_RATE / width * freq**2)
    step = (np.exp(1j * angle) / width) @ (factor[:, None] * np.exp(-1j * angle))
    right = np.block([[step.real, step.imag], [-step.imag, step.real]])
    right_high, right_low = halves(right)
    left_high, left_low = halves(right.T)
    right3 = np.concatenate([right_high, right_high, right_low], axis=0)
    left3 = np.concatenate([left_high, left_high, left_low], axis=1)
    left3 = left3.reshape(2, width // ROWS, ROWS, -1).swapaxes(0, 1).reshape(left3.shape)
    return right3, left3


def split(value):
    high = value.astype(jnp.bfloat16)
    low = (value - high.astype(jnp.float32)).astype(jnp.bfloat16)
    return high, low


def encode(real, imag, store):
    width = real.shape[0]
    codes = []
    for plane, value in enumerate((real, imag)):
        top = jnp.maximum(jnp.max(jnp.abs(value), axis=0, keepdims=True), 2.0**-100)
        code = jnp.ceil((jnp.log(top * (1.0 / 32766.0)) * (256.0 / math.log(2.0))))
        store(plane * width, jnp.round(value * jnp.exp2(code * (-1.0 / 256.0))).astype(jnp.int32).astype(jnp.int16))
        codes.append(code)
    return codes


def extra_rows(codes, places):
    width = codes[0].shape[1]
    rows = [
        jnp.broadcast_to(codes[0], (PLACES, width)),
        jnp.broadcast_to(places, (EXTRA // 2 - PLACES, width)),
        jnp.broadcast_to(codes[1], (EXTRA // 2, width)),
    ]
    return jnp.concatenate(rows, axis=0).astype(jnp.int32).astype(jnp.int16)


def decode(load, width):
    scales = jnp.exp2(load(2 * width, EXTRA).astype(jnp.int32).astype(jnp.float32) * (1.0 / 256.0))
    real = load(0, width).astype(jnp.int32).astype(jnp.float32) * scales[0:1]
    imag = load(width, width).astype(jnp.int32).astype(jnp.float32) * scales[EXTRA // 2 : EXTRA // 2 + 1]
    return real, imag


def nth_of_tile(tile_of, count, slots, tile, nth):
    found = jnp.int32(-1)
    seen = jnp.int32(0)
    for p in range(slots):
        hit = (tile_of(p) == tile) & (p < count)
        found = jnp.where(hit & (seen == nth), p, found)
        seen = seen + hit.astype(jnp.int32)
    return found


def batches():
    depth, depths = lax.axis_index("depth"), lax.axis_size("depth")
    latest = depths + STEPS - 2
    return latest - jnp.minimum(depth + STEPS - 1, depths - 1), latest - lax.rem(depth + 1, depths)


def prep_kernel(slab_ref, right_ref, left_ref, probe_ref, *refs):
    copies = [
        pltpu.make_async_copy(source, target, refs[4].at[n])
        for n, (source, target) in enumerate(zip((slab_ref, right_ref, left_ref, probe_ref), refs[:4]))
    ]
    for copy in copies:
        copy.start()
    for copy in copies:
        copy.wait()


def pack_kernel(tiles, pair, list_ref, count_ref, fronts_ref, *refs):
    out_refs = refs[:tiles]
    front_ref, in_sems = refs[tiles:]
    slots, _, width, _ = fronts_ref.shape
    own = lax.axis_index("tile")
    starting = batches()[0]

    def fetch(p):
        return pltpu.make_async_copy(fronts_ref.at[p], front_ref.at[p], in_sems.at[p])

    for p in range(slots):
        pl.when(p < count_ref[0, starting])(lambda p=p: fetch(p).start())
    chosen = {}
    for k in range(tiles):
        tile = lax.rem(own + k, tiles)
        for i in range(pair):
            for b, batch in enumerate(batches()):
                chosen[k, i, b] = nth_of_tile(
                    lambda p: list_ref[0, 0, p, batch], count_ref[0, batch], slots, tile, i
                )
    for p in range(slots):
        pl.when(p < count_ref[0, starting])(lambda p=p: fetch(p).wait())
    lane = lax.broadcasted_iota(jnp.int32, (1, width), 1)
    for k in list(range(1, tiles)) + [0]:
        for i in range(pair):
            places = jnp.zeros((1, width), jnp.int32)
            for b, batch in enumerate(batches()):
                p = chosen[k, i, b]
                live = (p >= 0).astype(jnp.int32)
                at = jnp.maximum(p, 0)
                values = (live, list_ref[0, 1, at, batch], list_ref[0, 2, at, batch])
                for offset, value in enumerate(values):
                    places = jnp.where(lane == 3 * b + offset, value, places)
            places = places.astype(jnp.float32)
            p = chosen[k, i, 0]

            def store(row, block):
                out_refs[k][i, row : row + block.shape[0], :] = block

            @pl.when(p >= 0)
            def _():
                store(2 * width, extra_rows(encode(front_ref[p, 0], front_ref[p, 1], store), places))

            @pl.when(p < 0)
            def _():
                none = jnp.zeros((1, width), jnp.float32)
                store(2 * width, extra_rows((none, none), places))


def unpack_kernel(tiles, pair, ks, first, list_ref, count_ref, *refs):
    in_refs, (out_ref, exit_ref, out_sems) = refs[: len(ks)], refs[-3:]
    slots, _, width, _ = out_ref.shape
    own = lax.axis_index("tile")
    batch = lax.axis_size("depth") + STEPS - 2 - lax.axis_index("depth")
    count = count_ref[0, batch]

    def send(p):
        return pltpu.make_async_copy(exit_ref.at[p], out_ref.at[p], out_sems.at[p])

    if first:
        for p in range(slots):

            @pl.when(p >= count)
            def _():
                exit_ref[p] = jnp.zeros(exit_ref.shape[1:], jnp.float32)
                send(p).start()

    found = []
    for n, k in enumerate(ks):
        tile = lax.rem(own + k, tiles)
        for i in range(pair):
            p = nth_of_tile(lambda p: list_ref[0, 0, p, batch], count, slots, tile, i)
            found.append(p)

            @pl.when(p >= 0)
            def _():
                real, imag = decode(lambda row, size: in_refs[n][i, row : row + size, :], width)
                exit_ref[p, 0] = real
                exit_ref[p, 1] = imag
                send(p).start()

    for p in found:
        pl.when(p >= 0)(lambda p=p: send(p).wait())
    if first:
        for p in range(slots):
            pl.when(p >= count)(lambda p=p: send(p).wait())


def cut(slab_ref, layer, row, column, patch_ref):
    width, side = patch_ref.shape[-1], slab_ref.shape[-1]
    block = jnp.minimum(column // width, side // width - 2)
    shift = column - block * width
    start = pl.multiple_of(row - row_offset(row, width, side), SPAN)
    rows = width + SPAN
    lane = lax.broadcasted_iota(jnp.int32, (rows, width), 1)
    turn = lax.rem(width - shift, width)
    for plane in range(2):
        parts = []
        for b in range(2):
            lanes = pl.ds(pl.multiple_of((block + b) * width, width), width)
            parts.append(pltpu.roll(slab_ref[layer, plane, pl.ds(start, rows), lanes], turn, 1))
        patch_ref[plane] = jnp.where(lane < width - shift, parts[0], parts[1]).astype(jnp.float32)


def row_offset(row, width, side):
    return row - jnp.minimum((row // SPAN) * SPAN, side - width - SPAN)


def run_layers(steps, places, wave_ref, patch_ref, x_refs, y_refs, right_ref, left_ref):
    width = wave_ref.shape[1] // 2
    side = steps[0][0].shape[-1]

    def fill(which, turn, pair):
        slab_ref, layer, _ = steps[which]
        for w in (2 * pair, 2 * pair + 1):
            cut(slab_ref, layer, *places[w], patch_ref.at[turn, w])

    def multiply(which, pair, n, first_row, real, imag):
        turn = which % 2
        w = 2 * pair + n
        start = row_offset(places[w][0], width, side) + first_row
        part = pl.ds(start, real.shape[0])
        trans_real, trans_imag = patch_ref[turn, w, 0, part, :], patch_ref[turn, w, 1, part, :]
        rows = slice(n * width + first_row, n * width + first_row + real.shape[0])
        for plane, value in enumerate((real * trans_real - imag * trans_imag, real * trans_imag + imag * trans_real)):
            high, low = split(value)
            x_refs[pair][rows, plane * width : (plane + 1) * width] = high
            x_refs[pair][rows, (2 + plane) * width : (3 + plane) * width] = low

    def enter(which, pair):
        for n in range(2):
            rows = slice((2 * pair + n) * width, (2 * pair + n + 1) * width)
            multiply(which, pair, n, 0, wave_ref[rows, :width], wave_ref[rows, width:])

    def right(pair):
        spreads = []
        for n in range(2):
            x = x_refs[pair][n * width : (n + 1) * width]
            x = jnp.concatenate([x, x[:, : 2 * width]], axis=1)
            spreads.append(jnp.dot(x, right_ref[...], preferred_element_type=jnp.float32))
        for n, spread in enumerate(spreads):
            lanes = slice(n * width, (n + 1) * width)
            for b in range(width // ROWS):
                for plane in range(2):
                    rows = slice(b * ROWS, (b + 1) * ROWS)
                    high, low = split(spread[rows, plane * width : (plane + 1) * width])
                    start = plane * width + b * ROWS
                    y_refs[pair][start : start + ROWS, lanes] = high
                    y_refs[pair][2 * width + start : 2 * width + start + ROWS, lanes] = low

    def left(pair, ahead):
        y = y_refs[pair][...]
        y = jnp.concatenate([y, y[: 2 * width]], axis=0)
        outs = [
            jnp.dot(left_ref[half * width : (half + 1) * width], y, preferred_element_type=jnp.float32)
            for half in range(2)
        ]
        for b in range(width // ROWS):
            out, c = outs[2 * b // (width // ROWS)], b % (width // ROWS // 2)
            for n in range(2):
                lanes = slice(n * width, (n + 1) * width)
                real = out[2 * c * ROWS : (2 * c + 1) * ROWS, lanes]
                imag = out[(2 * c + 1) * ROWS : (2 * c + 2) * ROWS, lanes]
                if ahead is None:
                    rows = slice((2 * pair + n) * width + b * ROWS, (2 * pair + n) * width + (b + 1) * ROWS)
                    wave_ref[rows, :width] = real
                    wave_ref[rows, width:] = imag
                else:
                    multiply(ahead, pair, n, b * ROWS, real, imag)

    def one(which, ends):
        for pair in range(GROUP // 2):
            right(pair)
            if which + 1 < len(steps):
                fill(which + 1, 1 - which % 2, pair)
        for pair in range(GROUP // 2):
            left(pair, None if ends else which + 1)

    which = 0
    while which < len(steps):
        condition = steps[which][2]
        block = [which]
        while block[-1] + 1 < len(steps) and steps[block[-1] + 1][2] is condition:
            block.append(block[-1] + 1)

        def run(block=tuple(block)):
            if block[0] == 0:
                for pair in range(GROUP // 2):
                    fill(0, 0, pair)
            for pair in range(GROUP // 2):
                enter(block[0], pair)
            for step in block:
                one(step, step == block[-1])

        if condition is None:
            run()
        else:
            pl.when(condition)(run)
            later = block[-1] + 1
            if later < len(steps):

                def skip(later=later):
                    for pair in range(GROUP // 2):
                        fill(later, later % 2, pair)

                pl.when(jnp.logical_not(condition))(skip)
        which = block[-1] + 1


def read_places(in_refs, b, pair, column_ref, place_ref, sem):
    for n, ref in enumerate(in_refs):
        for i in range(pair):
            rows = ref[i, ref.shape[1] - EXTRA :, :].astype(jnp.int32)
            column_ref[n * pair + i : n * pair + i + 1, :] = rows[PLACES : PLACES + 1]
    copy = pltpu.make_async_copy(column_ref, place_ref, sem)
    copy.start()
    copy.wait()
    live, places = [], []
    for j in range(len(in_refs) * pair):
        on = place_ref[j, 3 * b]
        live.append(on == 1)
        places.append((place_ref[j, 3 * b + 1] * on, place_ref[j, 3 * b + 2] * on))
    return live, places


def wave_to(ref, j, width, real, imag):
    rows = slice(j * width, (j + 1) * width)
    ref[rows, :width] = real
    ref[rows, width:] = imag


def send_wave(wave_ref, j, width, ref, at):
    rows = slice(j * width, (j + 1) * width)

    def store(row, block):
        ref[at, row : row + block.shape[0], :] = block

    codes = encode(wave_ref[rows, :width], wave_ref[rows, width:], store)
    store(2 * width, extra_rows(codes, jnp.zeros((1, width), jnp.float32)))


def first_kernel(ks, pair, own_ref, next_ref, right_ref, left_ref, *refs):
    in_refs, move_ref = refs[: len(ks)], refs[len(ks)]
    column_ref, place_ref, sem, wave_ref, patch_ref, *buffers = refs[len(ks) + 1 :]
    width = right_ref.shape[1] // 2
    depth, depths = lax.axis_index("depth"), lax.axis_size("depth")
    live, places = read_places(in_refs, 0, pair, column_ref, place_ref, sem)
    some = functools.reduce(jnp.logical_or, live)

    @pl.when(some & (depth + STEPS - 1 < depths))
    def _():
        for j in range(GROUP):
            source = in_refs[j // pair]
            wave_to(wave_ref, j, width, *decode(lambda row, size: source[j % pair, row : row + size, :], width))
        even = lax.rem(depth, 2) == 0
        steps = [(own_ref, 0, None), (own_ref, 1, None), (next_ref, 0, even), (next_ref, 1, even)]
        run_layers(steps, places, wave_ref, patch_ref, buffers[:2], buffers[2:], right_ref, left_ref)
        for j in range(GROUP):
            pl.when(live[j])(lambda j=j: send_wave(wave_ref, j, width, move_ref, j))


def second_kernel(ks, pair, last_ref, own_ref, next_ref, probe_ref, right_ref, left_ref, arrived_ref, *refs):
    in_refs, out_refs = refs[: len(ks)], refs[len(ks) : 2 * len(ks)]
    column_ref, place_ref, sem, wave_ref, patch_ref, *buffers = refs[2 * len(ks) :]
    width = right_ref.shape[1] // 2
    depth, depths = lax.axis_index("depth"), lax.axis_size("depth")
    live, places = read_places(in_refs, 1, pair, column_ref, place_ref, sem)
    some = functools.reduce(jnp.logical_or, live)

    @pl.when(some)
    def _():
        final = depth == depths - 1
        fresh = jnp.logical_or(depth < 2, final)
        for j in range(GROUP):

            @pl.when(fresh)
            def _():
                wave_to(wave_ref, j, width, probe_ref[0], probe_ref[1])

            @pl.when(jnp.logical_not(fresh))
            def _():
                wave_to(wave_ref, j, width, *decode(lambda row, size: arrived_ref[j, row : row + size, :], width))

        inner = jnp.logical_not(final)
        below = inner & (lax.rem(depth, 2) == 1)
        steps = [(last_ref, 0, below), (last_ref, 1, below), (own_ref, 0, inner), (own_ref, 1, inner)]
        steps += [(next_ref, 0, None), (next_ref, 1, None)]
        run_layers(steps, places, wave_ref, patch_ref, buffers[:2], buffers[2:], right_ref, left_ref)
        for j in range(GROUP):
            pl.when(live[j])(lambda j=j: send_wave(wave_ref, j, width, out_refs[j // pair], j % pair))


def on_chip(value):
    return pltpu.with_memory_space_constraint(value, pltpu.MemorySpace.VMEM)


def off_chip(value):
    return pltpu.with_memory_space_constraint(value, pltpu.MemorySpace.HBM)


def per_device(fronts, probe_wave, object_slices, patch_list, counts):
    depths = lax.axis_size("depth")
    tiles = lax.axis_size("tile")
    slots = fronts.shape[2]
    width = fronts.shape[-1]
    pair = slots // tiles
    per_group = GROUP // pair
    groups = [tuple(range(g, g + per_group)) for g in range(0, tiles, per_group)][::-1]
    right3, left3 = (jnp.asarray(table) for table in propagators(width))
    coded_rows = 2 * width + EXTRA
    coded = pltpu.VMEM((pair, coded_rows, width), jnp.int16)
    lists = [jnp.transpose(patch_list, (1, 2, 3, 0)), jnp.transpose(counts)]
    lists = [off_chip(value) for value in lists]

    next_slab = on_chip(lax.ppermute(object_slices, "depth", [((d + 1) % depths, d) for d in range(depths)]))
    last_slab = on_chip(lax.ppermute(object_slices, "depth", [(d, d + 1) for d in range(0, depths, 2)]))
    packed = pl.pallas_call(
        functools.partial(pack_kernel, tiles, pair),
        out_shape=[coded] * tiles,
        in_specs=[SMEM, SMEM, HBM],
        out_specs=[VMEM] * tiles,
        scratch_shapes=[pltpu.VMEM(fronts.shape[2:], jnp.float32), pltpu.SemaphoreType.DMA((slots,))],
        compiler_params=PARAMS,
        name="pack",
    )(*lists, off_chip(fronts[0, 0]))
    kept = (object_slices, right3, left3, probe_wave)
    own_slab, right, left, probe = pl.pallas_call(
        prep_kernel,
        out_shape=[pltpu.VMEM(value.shape, value.dtype) for value in kept],
        in_specs=[HBM] * 4,
        out_specs=[VMEM] * 4,
        scratch_shapes=[pltpu.SemaphoreType.DMA((4,))],
        compiler_params=PARAMS,
        name="prep",
    )(*[off_chip(value) for value in kept])

    def flat(depth, tile):
        return (depth % depths) * tiles + tile % tiles

    def turned(k):
        return [(t, (t + k) % tiles) for t in range(tiles)]

    brought = [packed[0]]
    for k in range(1, tiles):
        brought.append(on_chip(lax.ppermute(packed[k], "tile", turned(k))))
    scratch = [
        pltpu.VMEM((8, width), jnp.int32),
        pltpu.SMEM((8, width), jnp.int32),
        pltpu.SemaphoreType.DMA,
        pltpu.VMEM((GROUP * width, 2 * width), jnp.float32),
        pltpu.VMEM((2, GROUP, 2, width + SPAN, width), jnp.float32),
        *[pltpu.VMEM((2 * width, 4 * width), jnp.bfloat16)] * (GROUP // 2),
        *[pltpu.VMEM((4 * width, 2 * width), jnp.bfloat16)] * (GROUP // 2),
    ]
    moved_shape = pltpu.VMEM((GROUP, coded_rows, width), jnp.int16)
    flops = 2 * GROUP * (2 * 3) * width * (2 * width) ** 2
    arrived = []
    for ks in groups:
        moved = pl.pallas_call(
            functools.partial(first_kernel, ks, pair),
            out_shape=moved_shape,
            in_specs=[VMEM] * (4 + per_group),
            out_specs=VMEM,
            scratch_shapes=scratch,
            cost_estimate=pl.CostEstimate(flops=4 * flops, bytes_accessed=0, transcendentals=0),
            compiler_params=PARAMS,
        )(own_slab, next_slab, right, left, *[brought[k] for k in ks])
        pairs = [(d, d + 2) for d in range(depths - STEPS + 1)]
        arrived.append(on_chip(lax.ppermute(moved, "depth", pairs)))
    back = [None] * tiles
    for g, ks in enumerate(groups):
        outs = pl.pallas_call(
            functools.partial(second_kernel, ks, pair),
            out_shape=[coded] * per_group,
            in_specs=[VMEM] * (7 + per_group),
            out_specs=[VMEM] * per_group,
            scratch_shapes=scratch,
            cost_estimate=pl.CostEstimate(flops=4 * flops, bytes_accessed=0, transcendentals=0),
            compiler_params=PARAMS,
        )(last_slab, own_slab, next_slab, probe, right, left, arrived[g], *[brought[k] for k in ks])
        for k, value in zip(ks, outs):
            pairs = [(flat(d, t), flat(d + 1, t - k)) for d in range(depths) for t in range(tiles)]
            back[k] = on_chip(lax.ppermute(value, ("depth", "tile"), pairs))
    exits = None
    for g, ks in enumerate(groups):
        before = [] if exits is None else [exits]
        exits = pl.pallas_call(
            functools.partial(unpack_kernel, tiles, pair, ks, g == 0),
            out_shape=jax.ShapeDtypeStruct(fronts.shape[2:], jnp.float32),
            in_specs=[SMEM, SMEM] + [VMEM] * per_group + [HBM] * len(before),
            out_specs=HBM,
            input_output_aliases={2 + per_group: 0} if before else {},
            scratch_shapes=[pltpu.VMEM(fronts.shape[2:], jnp.float32), pltpu.SemaphoreType.DMA((slots,))],
            compiler_params=PARAMS,
        )(*lists, *[back[k] for k in ks], *before)
    return exits[None, None]


def solution(mesh):
    in_specs = (
        P("depth", "tile", None, None, None, None),
        P(),
        P("depth", None, "tile", None),
        P(None, "tile", None, None),
        P(None, "tile"),
    )
    out_specs = P("depth", "tile", None, None, None, None)

    return jax.shard_map(per_device, mesh=mesh, in_specs=in_specs, out_specs=out_specs, check_vma=False)
```

```python
import functools
import math

import jax
import jax.numpy as jnp
import ml_dtypes
import numpy as np
from jax import lax
from jax.experimental import pallas as pl
from jax.experimental.pallas import tpu as pltpu
from jax.sharding import PartitionSpec as P


STEPS = 4
FRESNEL_RATE = 0.3
EXTRA = 16
PLACES = 4
SPAN = 16
ROWS = 16
GROUP = 4

HBM = pl.BlockSpec(memory_space=pltpu.MemorySpace.HBM)
VMEM = pl.BlockSpec(memory_space=pltpu.VMEM)
PARAMS = pltpu.CompilerParams(vmem_limit_bytes=24 * 2**20)


def halves(table):
    high = table.astype(ml_dtypes.bfloat16)
    low = (table - high.astype(np.float64)).astype(ml_dtypes.bfloat16)
    return high, low


@functools.lru_cache(None)
def propagators(width):
    index = np.arange(width)
    angle = 2.0 * np.pi * ((index[:, None] * index[None, :]) % width) / width
    freq = np.where(index < width // 2, index, index - width).astype(np.float64)
    factor = np.exp(-2j * np.pi * FRESNEL_RATE / width * freq**2)
    step = (np.exp(1j * angle) / width) @ (factor[:, None] * np.exp(-1j * angle))
    right = np.block([[step.real, step.imag], [-step.imag, step.real]])
    right_high, right_low = halves(right)
    left_high, left_low = halves(right.T)
    right3 = np.concatenate([right_high, right_high, right_low], axis=0)
    left3 = np.concatenate([left_high, left_high, left_low], axis=1)
    left3 = left3.reshape(2, width // ROWS, ROWS, -1).swapaxes(0, 1).reshape(left3.shape)
    return right3, left3


def split(value):
    high = value.astype(jnp.bfloat16)
    low = (value - high.astype(jnp.float32)).astype(jnp.bfloat16)
    return high, low


def encode(real, imag, store):
    width = real.shape[0]
    codes = []
    for plane, value in enumerate((real, imag)):
        top = jnp.maximum(jnp.max(jnp.abs(value), axis=0, keepdims=True), 2.0**-100)
        code = jnp.ceil((jnp.log(top * (1.0 / 32766.0)) * (256.0 / math.log(2.0))))
        store(plane * width, jnp.round(value * jnp.exp2(code * (-1.0 / 256.0))).astype(jnp.int32).astype(jnp.int16))
        codes.append(code)
    return codes


def extra_rows(codes, places):
    width = codes[0].shape[1]
    rows = [
        jnp.broadcast_to(codes[0], (PLACES, width)),
        jnp.broadcast_to(places, (EXTRA // 2 - PLACES, width)),
        jnp.broadcast_to(codes[1], (EXTRA // 2, width)),
    ]
    return jnp.concatenate(rows, axis=0).astype(jnp.int32).astype(jnp.int16)


def decode(load, width):
    scales = jnp.exp2(load(2 * width, EXTRA).astype(jnp.int32).astype(jnp.float32) * (1.0 / 256.0))
    real = load(0, width).astype(jnp.int32).astype(jnp.float32) * scales[0:1]
    imag = load(width, width).astype(jnp.int32).astype(jnp.float32) * scales[EXTRA // 2 : EXTRA // 2 + 1]
    return real, imag


def nth_of_tile(tile_of, count, slots, tile, nth):
    found = jnp.int32(-1)
    seen = jnp.int32(0)
    for p in range(slots):
        hit = (tile_of(p) == tile) & (p < count)
        found = jnp.where(hit & (seen == nth), p, found)
        seen = seen + hit.astype(jnp.int32)
    return found


def batches():
    depth, depths = lax.axis_index("depth"), lax.axis_size("depth")
    latest = depths + STEPS - 2
    return latest - jnp.minimum(depth + STEPS - 1, depths - 1), latest - lax.rem(depth + 1, depths)


def prep_kernel(slab_ref, right_ref, left_ref, probe_ref, *refs):
    copies = [
        pltpu.make_async_copy(source, target, refs[4].at[n])
        for n, (source, target) in enumerate(zip((slab_ref, right_ref, left_ref, probe_ref), refs[:4]))
    ]
    for copy in copies:
        copy.start()
    for copy in copies:
        copy.wait()


def pack_kernel(tiles, pair, lists_ref, counts_ref, fronts_ref, *refs):
    out_refs = refs[:tiles]
    front_ref, in_sems, list_ref, count_ref, list_sems = refs[tiles:]
    slots, _, width, _ = fronts_ref.shape
    own = lax.axis_index("tile")

    def fetch(p):
        return pltpu.make_async_copy(fronts_ref.at[p], front_ref.at[p], in_sems.at[p])

    lists = [
        pltpu.make_async_copy(lists_ref, list_ref, list_sems.at[0]),
        pltpu.make_async_copy(counts_ref, count_ref, list_sems.at[1]),
    ]
    for copy in lists:
        copy.start()
    for p in range(slots):
        fetch(p).start()
    for copy in lists:
        copy.wait()
    chosen = {}
    for k in range(tiles):
        tile = lax.rem(own + k, tiles)
        for i in range(pair):
            for b, batch in enumerate(batches()):
                chosen[k, i, b] = nth_of_tile(
                    lambda p: list_ref[0, 0, p, batch], count_ref[0, batch], slots, tile, i
                )
    for p in range(slots):
        fetch(p).wait()
    lane = lax.broadcasted_iota(jnp.int32, (1, width), 1)
    for k in list(range(1, tiles)) + [0]:
        for i in range(pair):
            places = jnp.zeros((1, width), jnp.int32)
            for b, batch in enumerate(batches()):
                p = chosen[k, i, b]
                live = (p >= 0).astype(jnp.int32)
                at = jnp.maximum(p, 0)
                values = (live, list_ref[0, 1, at, batch], list_ref[0, 2, at, batch])
                for offset, value in enumerate(values):
                    places = jnp.where(lane == 3 * b + offset, value, places)
            places = places.astype(jnp.float32)
            p = chosen[k, i, 0]

            def store(row, block):
                out_refs[k][i, row : row + block.shape[0], :] = block

            @pl.when(p >= 0)
            def _():
                store(2 * width, extra_rows(encode(front_ref[p, 0], front_ref[p, 1], store), places))

            @pl.when(p < 0)
            def _():
                none = jnp.zeros((1, width), jnp.float32)
                store(2 * width, extra_rows((none, none), places))


def unpack_kernel(tiles, pair, ks, first, lists_ref, counts_ref, *refs):
    in_refs, (out_ref, exit_ref, out_sems, list_ref, count_ref, list_sems) = refs[: len(ks)], refs[-6:]
    lists = [
        pltpu.make_async_copy(lists_ref, list_ref, list_sems.at[0]),
        pltpu.make_async_copy(counts_ref, count_ref, list_sems.at[1]),
    ]
    for copy in lists:
        copy.start()
    for copy in lists:
        copy.wait()
    slots, _, width, _ = out_ref.shape
    own = lax.axis_index("tile")
    batch = lax.axis_size("depth") + STEPS - 2 - lax.axis_index("depth")
    count = count_ref[0, batch]

    def send(p):
        return pltpu.make_async_copy(exit_ref.at[p], out_ref.at[p], out_sems.at[p])

    if first:
        for p in range(slots):

            @pl.when(p >= count)
            def _():
                exit_ref[p] = jnp.zeros(exit_ref.shape[1:], jnp.float32)
                send(p).start()

    found = []
    for n, k in enumerate(ks):
        tile = lax.rem(own + k, tiles)
        for i in range(pair):
            p = nth_of_tile(lambda p: list_ref[0, 0, p, batch], count, slots, tile, i)
            found.append(p)

            @pl.when(p >= 0)
            def _():
                real, imag = decode(lambda row, size: in_refs[n][i, row : row + size, :], width)
                exit_ref[p, 0] = real
                exit_ref[p, 1] = imag
                send(p).start()

    for p in found:
        pl.when(p >= 0)(lambda p=p: send(p).wait())
    if first:
        for p in range(slots):
            pl.when(p >= count)(lambda p=p: send(p).wait())


def cut(slab_ref, layer, row, column, patch_ref):
    width, side = patch_ref.shape[-1], slab_ref.shape[-1]
    block = jnp.minimum(column // width, side // width - 2)
    shift = column - block * width
    start = pl.multiple_of(row - row_offset(row, width, side), SPAN)
    rows = width + SPAN
    lane = lax.broadcasted_iota(jnp.int32, (rows, width), 1)
    turn = lax.rem(width - shift, width)
    for plane in range(2):
        parts = []
        for b in range(2):
            lanes = pl.ds(pl.multiple_of((block + b) * width, width), width)
            parts.append(pltpu.roll(slab_ref[layer, plane, pl.ds(start, rows), lanes], turn, 1))
        patch_ref[plane] = jnp.where(lane < width - shift, parts[0], parts[1]).astype(jnp.float32)


def row_offset(row, width, side):
    return row - jnp.minimum((row // SPAN) * SPAN, side - width - SPAN)


def run_layers(steps, places, wave_ref, patch_ref, x_refs, y_refs, right_ref, left_ref):
    width = wave_ref.shape[1] // 2
    side = steps[0][0].shape[-1]

    def fill(which, turn, pair):
        slab_ref, layer, _ = steps[which]
        for w in (2 * pair, 2 * pair + 1):
            cut(slab_ref, layer, *places[w], patch_ref.at[turn, w])

    def multiply(which, pair, n, first_row, real, imag):
        turn = which % 2
        w = 2 * pair + n
        start = row_offset(places[w][0], width, side) + first_row
        part = pl.ds(start, real.shape[0])
        trans_real, trans_imag = patch_ref[turn, w, 0, part, :], patch_ref[turn, w, 1, part, :]
        rows = slice(n * width + first_row, n * width + first_row + real.shape[0])
        for plane, value in enumerate((real * trans_real - imag * trans_imag, real * trans_imag + imag * trans_real)):
            high, low = split(value)
            x_refs[pair][rows, plane * width : (plane + 1) * width] = high
            x_refs[pair][rows, (2 + plane) * width : (3 + plane) * width] = low

    def enter(which, pair):
        for n in range(2):
            rows = slice((2 * pair + n) * width, (2 * pair + n + 1) * width)
            multiply(which, pair, n, 0, wave_ref[rows, :width], wave_ref[rows, width:])

    def right(pair):
        spreads = []
        for n in range(2):
            x = x_refs[pair][n * width : (n + 1) * width]
            x = jnp.concatenate([x, x[:, : 2 * width]], axis=1)
            spreads.append(jnp.dot(x, right_ref[...], preferred_element_type=jnp.float32))
        for n, spread in enumerate(spreads):
            lanes = slice(n * width, (n + 1) * width)
            for b in range(width // ROWS):
                for plane in range(2):
                    rows = slice(b * ROWS, (b + 1) * ROWS)
                    high, low = split(spread[rows, plane * width : (plane + 1) * width])
                    start = plane * width + b * ROWS
                    y_refs[pair][start : start + ROWS, lanes] = high
                    y_refs[pair][2 * width + start : 2 * width + start + ROWS, lanes] = low

    def left(pair, ahead):
        y = y_refs[pair][...]
        y = jnp.concatenate([y, y[: 2 * width]], axis=0)
        outs = [
            jnp.dot(left_ref[half * width : (half + 1) * width], y, preferred_element_type=jnp.float32)
            for half in range(2)
        ]
        for b in range(width // ROWS):
            out, c = outs[2 * b // (width // ROWS)], b % (width // ROWS // 2)
            for n in range(2):
                lanes = slice(n * width, (n + 1) * width)
                real = out[2 * c * ROWS : (2 * c + 1) * ROWS, lanes]
                imag = out[(2 * c + 1) * ROWS : (2 * c + 2) * ROWS, lanes]
                if ahead is None:
                    rows = slice((2 * pair + n) * width + b * ROWS, (2 * pair + n) * width + (b + 1) * ROWS)
                    wave_ref[rows, :width] = real
                    wave_ref[rows, width:] = imag
                else:
                    multiply(ahead, pair, n, b * ROWS, real, imag)

    def one(which, ends):
        for pair in range(GROUP // 2):
            right(pair)
            if which + 1 < len(steps):
                fill(which + 1, 1 - which % 2, pair)
        for pair in range(GROUP // 2):
            left(pair, None if ends else which + 1)

    which = 0
    while which < len(steps):
        condition = steps[which][2]
        block = [which]
        while block[-1] + 1 < len(steps) and steps[block[-1] + 1][2] is condition:
            block.append(block[-1] + 1)

        def run(block=tuple(block)):
            if block[0] == 0:
                for pair in range(GROUP // 2):
                    fill(0, 0, pair)
            for pair in range(GROUP // 2):
                enter(block[0], pair)
            for step in block:
                one(step, step == block[-1])

        if condition is None:
            run()
        else:
            pl.when(condition)(run)
            later = block[-1] + 1
            if later < len(steps):

                def skip(later=later):
                    for pair in range(GROUP // 2):
                        fill(later, later % 2, pair)

                pl.when(jnp.logical_not(condition))(skip)
        which = block[-1] + 1


def read_places(in_refs, b, pair, column_ref, place_ref, sem):
    for n, ref in enumerate(in_refs):
        for i in range(pair):
            rows = ref[i, ref.shape[1] - EXTRA :, :].astype(jnp.int32)
            column_ref[n * pair + i : n * pair + i + 1, :] = rows[PLACES : PLACES + 1]
    copy = pltpu.make_async_copy(column_ref, place_ref, sem)
    copy.start()
    copy.wait()
    live, places = [], []
    for j in range(len(in_refs) * pair):
        on = place_ref[j, 3 * b]
        live.append(on == 1)
        places.append((place_ref[j, 3 * b + 1] * on, place_ref[j, 3 * b + 2] * on))
    return live, places


def wave_to(ref, j, width, real, imag):
    rows = slice(j * width, (j + 1) * width)
    ref[rows, :width] = real
    ref[rows, width:] = imag


def send_wave(wave_ref, j, width, ref, at):
    rows = slice(j * width, (j + 1) * width)

    def store(row, block):
        ref[at, row : row + block.shape[0], :] = block

    codes = encode(wave_ref[rows, :width], wave_ref[rows, width:], store)
    store(2 * width, extra_rows(codes, jnp.zeros((1, width), jnp.float32)))


def first_kernel(ks, pair, own_ref, next_ref, right_ref, left_ref, *refs):
    in_refs, move_ref = refs[: len(ks)], refs[len(ks)]
    column_ref, place_ref, sem, wave_ref, patch_ref, *buffers = refs[len(ks) + 1 :]
    width = right_ref.shape[1] // 2
    depth, depths = lax.axis_index("depth"), lax.axis_size("depth")
    live, places = read_places(in_refs, 0, pair, column_ref, place_ref, sem)
    some = functools.reduce(jnp.logical_or, live)

    @pl.when(some & (depth + STEPS - 1 < depths))
    def _():
        for j in range(GROUP):
            source = in_refs[j // pair]
            wave_to(wave_ref, j, width, *decode(lambda row, size: source[j % pair, row : row + size, :], width))
        even = lax.rem(depth, 2) == 0
        steps = [(own_ref, 0, None), (own_ref, 1, None), (next_ref, 0, even), (next_ref, 1, even)]
        run_layers(steps, places, wave_ref, patch_ref, buffers[:2], buffers[2:], right_ref, left_ref)
        for j in range(GROUP):
            pl.when(live[j])(lambda j=j: send_wave(wave_ref, j, width, move_ref, j))


def second_kernel(ks, pair, last_ref, own_ref, next_ref, probe_ref, right_ref, left_ref, arrived_ref, *refs):
    in_refs, out_refs = refs[: len(ks)], refs[len(ks) : 2 * len(ks)]
    column_ref, place_ref, sem, wave_ref, patch_ref, *buffers = refs[2 * len(ks) :]
    width = right_ref.shape[1] // 2
    depth, depths = lax.axis_index("depth"), lax.axis_size("depth")
    live, places = read_places(in_refs, 1, pair, column_ref, place_ref, sem)
    some = functools.reduce(jnp.logical_or, live)

    @pl.when(some)
    def _():
        final = depth == depths - 1
        fresh = jnp.logical_or(depth < 2, final)
        for j in range(GROUP):

            @pl.when(fresh)
            def _():
                wave_to(wave_ref, j, width, probe_ref[0], probe_ref[1])

            @pl.when(jnp.logical_not(fresh))
            def _():
                wave_to(wave_ref, j, width, *decode(lambda row, size: arrived_ref[j, row : row + size, :], width))

        inner = jnp.logical_not(final)
        below = inner & (lax.rem(depth, 2) == 1)
        steps = [(last_ref, 0, below), (last_ref, 1, below), (own_ref, 0, inner), (own_ref, 1, inner)]
        steps += [(next_ref, 0, None), (next_ref, 1, None)]
        run_layers(steps, places, wave_ref, patch_ref, buffers[:2], buffers[2:], right_ref, left_ref)
        for j in range(GROUP):
            pl.when(live[j])(lambda j=j: send_wave(wave_ref, j, width, out_refs[j // pair], j % pair))


def on_chip(value):
    return pltpu.with_memory_space_constraint(value, pltpu.MemorySpace.VMEM)


def off_chip(value):
    return pltpu.with_memory_space_constraint(value, pltpu.MemorySpace.HBM)


def per_device(fronts, probe_wave, object_slices, patch_list, counts):
    depths = lax.axis_size("depth")
    tiles = lax.axis_size("tile")
    slots = fronts.shape[2]
    width = fronts.shape[-1]
    pair = slots // tiles
    per_group = GROUP // pair
    groups = [tuple(range(g, g + per_group)) for g in range(0, tiles, per_group)][::-1]
    right3, left3 = (jnp.asarray(table) for table in propagators(width))
    coded_rows = 2 * width + EXTRA
    coded = pltpu.VMEM((pair, coded_rows, width), jnp.int16)
    lists = [jnp.transpose(patch_list, (1, 2, 3, 0)), jnp.transpose(counts)]
    lists = [off_chip(value) for value in lists]

    next_slab = on_chip(lax.ppermute(object_slices, "depth", [((d + 1) % depths, d) for d in range(depths)]))
    last_slab = on_chip(lax.ppermute(object_slices, "depth", [(d, d + 1) for d in range(0, depths, 2)]))
    packed = pl.pallas_call(
        functools.partial(pack_kernel, tiles, pair),
        out_shape=[coded] * tiles,
        in_specs=[HBM, HBM, HBM],
        out_specs=[VMEM] * tiles,
        scratch_shapes=[
            pltpu.VMEM(fronts.shape[2:], jnp.float32),
            pltpu.SemaphoreType.DMA((slots,)),
            *[pltpu.SMEM(value.shape, jnp.int32) for value in lists],
            pltpu.SemaphoreType.DMA((2,)),
        ],
        compiler_params=PARAMS,
        name="pack",
    )(*lists, off_chip(fronts[0, 0]))
    kept = (object_slices, right3, left3, probe_wave)
    own_slab, right, left, probe = pl.pallas_call(
        prep_kernel,
        out_shape=[pltpu.VMEM(value.shape, value.dtype) for value in kept],
        in_specs=[HBM] * 4,
        out_specs=[VMEM] * 4,
        scratch_shapes=[pltpu.SemaphoreType.DMA((4,))],
        compiler_params=PARAMS,
        name="prep",
    )(*[off_chip(value) for value in kept])

    def flat(depth, tile):
        return (depth % depths) * tiles + tile % tiles

    def turned(k):
        return [(t, (t + k) % tiles) for t in range(tiles)]

    brought = [packed[0]]
    for k in range(1, tiles):
        brought.append(on_chip(lax.ppermute(packed[k], "tile", turned(k))))
    scratch = [
        pltpu.VMEM((8, width), jnp.int32),
        pltpu.SMEM((8, width), jnp.int32),
        pltpu.SemaphoreType.DMA,
        pltpu.VMEM((GROUP * width, 2 * width), jnp.float32),
        pltpu.VMEM((2, GROUP, 2, width + SPAN, width), jnp.float32),
        *[pltpu.VMEM((2 * width, 4 * width), jnp.bfloat16)] * (GROUP // 2),
        *[pltpu.VMEM((4 * width, 2 * width), jnp.bfloat16)] * (GROUP // 2),
    ]
    moved_shape = pltpu.VMEM((GROUP, coded_rows, width), jnp.int16)
    flops = 2 * GROUP * (2 * 3) * width * (2 * width) ** 2
    arrived = []
    for ks in groups:
        moved = pl.pallas_call(
            functools.partial(first_kernel, ks, pair),
            out_shape=moved_shape,
            in_specs=[VMEM] * (4 + per_group),
            out_specs=VMEM,
            scratch_shapes=scratch,
            cost_estimate=pl.CostEstimate(flops=4 * flops, bytes_accessed=0, transcendentals=0),
            compiler_params=PARAMS,
        )(own_slab, next_slab, right, left, *[brought[k] for k in ks])
        pairs = [(d, d + 2) for d in range(depths - STEPS + 1)]
        arrived.append(on_chip(lax.ppermute(moved, "depth", pairs)))
    back = [None] * tiles
    for g, ks in enumerate(groups):
        outs = pl.pallas_call(
            functools.partial(second_kernel, ks, pair),
            out_shape=[coded] * per_group,
            in_specs=[VMEM] * (7 + per_group),
            out_specs=[VMEM] * per_group,
            scratch_shapes=scratch,
            cost_estimate=pl.CostEstimate(flops=4 * flops, bytes_accessed=0, transcendentals=0),
            compiler_params=PARAMS,
        )(last_slab, own_slab, next_slab, probe, right, left, arrived[g], *[brought[k] for k in ks])
        for k, value in zip(ks, outs):
            pairs = [(flat(d, t), flat(d + 1, t - k)) for d in range(depths) for t in range(tiles)]
            back[k] = on_chip(lax.ppermute(value, ("depth", "tile"), pairs))
    exits = None
    for g, ks in enumerate(groups):
        before = [] if exits is None else [exits]
        exits = pl.pallas_call(
            functools.partial(unpack_kernel, tiles, pair, ks, g == 0),
            out_shape=jax.ShapeDtypeStruct(fronts.shape[2:], jnp.float32),
            in_specs=[HBM, HBM] + [VMEM] * per_group + [HBM] * len(before),
            out_specs=HBM,
            input_output_aliases={2 + per_group: 0} if before else {},
            scratch_shapes=[
                pltpu.VMEM(fronts.shape[2:], jnp.float32),
                pltpu.SemaphoreType.DMA((slots,)),
                *[pltpu.SMEM(value.shape, jnp.int32) for value in lists],
                pltpu.SemaphoreType.DMA((2,)),
            ],
            compiler_params=PARAMS,
        )(*lists, *[back[k] for k in ks], *before)
    return exits[None, None]


def solution(mesh):
    in_specs = (
        P("depth", "tile", None, None, None, None),
        P(),
        P("depth", None, "tile", None),
        P(None, "tile", None, None),
        P(None, "tile"),
    )
    out_specs = P("depth", "tile", None, None, None, None)

    return jax.shard_map(per_device, mesh=mesh, in_specs=in_specs, out_specs=out_specs, check_vma=False)
```
